256 devices in a mesh: grid: 4 (over x), span: 4 (over y), normal: 16 (over z, core).
Axes of the slice: x: 4, y: 4, z: 8, core: 2. Of those that a mesh axis runs over, the one named last changes fastest.
Arguments:
- state: float32 [5, 4, 256, 4096], P(None, 'grid', 'normal', 'span'), may hold values from -6 to 6
- iblank: int32 [4, 256, 4096], P('grid', 'normal', 'span'), may hold values 0 or 1
- flux: float32 [5, 5, 4], P(None, None, 'grid'), may hold values from -3 to 3
- left_vectors: float32 [5, 5, 4, 4096], P(None, None, 'grid', 'span')
- right_vectors: float32 [5, 5, 4, 4096], P(None, None, 'grid', 'span')
- low_one: float32 [5, 4, 256, 4096], P(None, 'grid', 'normal', 'span'), as said below
- low_two: float32 [5, 4, 256, 4096], P(None, 'grid', 'normal', 'span')
- up_one: float32 [5, 4, 256, 4096], P(None, 'grid', 'normal', 'span')
- up_two: float32 [5, 4, 256, 4096], P(None, 'grid', 'normal', 'span')
- pivot: float32 [5, 4, 256, 4096], P(None, 'grid', 'normal', 'span')
- donor_cells: int32 [8, 4, 384, 512], P(None, 'grid', 'normal', 'span'), may hold values from 0 to 16383
- donor_weights: float32 [8, 4, 384, 512], P(None, 'grid', 'normal', 'span'), as said below
- fringe_cells: int32 [4, 384, 512], P('grid', 'normal', 'span'), may hold values from 0 to 16383, as said below
- fringe_live: int32 [4, 384, 512], P('grid', 'normal', 'span'), may hold values from 0 to 1, as said below
Outputs:
- updated: float32 [5, 4, 256, 4096], P(None, 'grid', 'normal', 'span')
The draws below stay inside these ranges and needn't reach their ends.
Inputs may be any that keep to these rules, and one draw needn't show every extreme that they name: In every cell |low_one| + |low_two| < 1 and |up_one| + |up_two| < 1, with low_one and up_one negative. `donor_weights`: each slot's eight weights are the trilinear weights of a point in a unit cell: nonnegative, summing to one. `fringe_cells`: on one device, the 3072 slots name distinct local cells. `fringe_live`: within the slots of one source grid on one device, the first k blocks are live and the others not, k from 1 to 6, and 0 for a grid's own slots; on every device some source grid has all 6 blocks live.
All inputs are finite; a program needn't handle non-finite values. No bound on the sum of `iblank` on one device may be relied on, other than what follows from the above.
Results may differ from the reference program's by a relative error of at most 0.0003.
Values sent between devices are 32-bit elements; how exact they have to be, the bound alone decides.
A program may use at most 128 MiB of HBM per device.

```python
import jax
import jax.numpy as jnp
from jax import lax

CN = 16
CS = 1024
CAP = 6
BLOCK = 128
ITERS = 2
GRIDS = 4
NN = 256
NS = 4096
N_SPAN = 4
N_NORMAL = 16


def decay_rates(key):
    low_end = jnp.log(jnp.float32(0.015))
    high_end = jnp.log(jnp.float32(0.5))
    sample = jax.random.uniform(jax.random.fold_in(key, 101), (5, GRIDS, 1, NS), jnp.float32)
    return jnp.exp(low_end + (high_end - low_end) * sample)


def jittered(key, salt):
    return jax.random.uniform(jax.random.fold_in(key, salt), (5, GRIDS, NN, NS), jnp.float32, 0.5, 1.5)


def signed(key, salt):
    return jax.random.uniform(jax.random.fold_in(key, salt), (5, GRIDS, NN, NS), jnp.float32, -1.0, 1.0)


def draw_low_one(key, part):
    return -(1.0 - decay_rates(key) * jittered(key, 11))


def draw_low_two(key, part):
    return 0.4 * decay_rates(key) * jittered(key, 11) * signed(key, 13)


def draw_up_one(key, part):
    return -(1.0 - decay_rates(key) * jittered(key, 21))


def draw_up_two(key, part):
    return 0.4 * decay_rates(key) * jittered(key, 21) * signed(key, 23)


def draw_pivot(key, part):
    return decay_rates(key) * jittered(key, 31)


def dominant(key):
    first_key, second_key = jax.random.split(key)
    diagonal = jax.random.uniform(first_key, (5, 5, GRIDS, NS), jnp.float32, 0.8, 1.2)
    coupling = jax.random.uniform(second_key, (5, 5, GRIDS, NS), jnp.float32, -0.35, 0.35)
    identity = jnp.eye(5, dtype=jnp.float32)[:, :, None, None]
    return identity * diagonal + (1.0 - identity) * coupling


def draw_left_vectors(key, part):
    return dominant(jax.random.fold_in(key, 41))


def draw_right_vectors(key, part):
    return dominant(jax.random.fold_in(key, 43))


def draw_donor_weights(key, part):
    shape = (GRIDS, N_NORMAL * GRIDS * CAP, N_SPAN * BLOCK)
    fractions = jax.random.uniform(jax.random.fold_in(key, 51), (3,) + shape, jnp.float32)
    stacked = []
    for corner in range(8):
        weight = jnp.ones(shape, jnp.float32)
        for axis_bit in range(3):
            if corner >> axis_bit & 1:
                weight = weight * fractions[axis_bit]
            else:
                weight = weight * (1.0 - fractions[axis_bit])
        stacked.append(weight)
    return jnp.stack(stacked)


def draw_fringe_cells(key, part):
    devices = GRIDS * N_NORMAL * N_SPAN
    slot_count = GRIDS * CAP * BLOCK
    device_keys = jax.random.split(jax.random.fold_in(key, 61), devices)
    chosen = jax.vmap(lambda device_key: jax.random.permutation(device_key, CN * CS)[:slot_count])(device_keys)
    chosen = chosen.reshape(GRIDS, N_NORMAL, N_SPAN, GRIDS, CAP, BLOCK)
    return chosen.transpose(0, 1, 3, 4, 2, 5).reshape(GRIDS, N_NORMAL * GRIDS * CAP, N_SPAN * BLOCK).astype(jnp.int32)


def draw_fringe_live(key, part):
    counts = jax.random.randint(jax.random.fold_in(key, 71), (GRIDS, N_NORMAL, N_SPAN, GRIDS), 1, CAP + 1)
    receiver = jnp.arange(GRIDS)[:, None, None, None]
    source = jnp.arange(GRIDS)[None, None, None, :]
    counts = jnp.where(source == (receiver + 1) % GRIDS, CAP, counts)
    counts = jnp.where(source == receiver, 0, counts)
    block_index = jnp.arange(CAP)[None, None, None, None, :]
    live = (block_index < counts[..., None]).astype(jnp.int32)
    live = jnp.broadcast_to(live[..., None], (GRIDS, N_NORMAL, N_SPAN, GRIDS, CAP, BLOCK))
    return live.transpose(0, 1, 3, 4, 2, 5).reshape(GRIDS, N_NORMAL * GRIDS * CAP, N_SPAN * BLOCK).astype(jnp.int32)


def touch_ends(array, key, least, largest):
    longest = array.shape.index(max(array.shape))
    spots = []
    for shift in (0, 1):
        where = [jax.random.randint(jax.random.fold_in(key, axis), (), 0, length) for axis, length in enumerate(array.shape)]
        where[longest] = (where[longest] + shift) % array.shape[longest]
        spots.append(tuple(where))
    return array.at[spots[0]].set(least).at[spots[1]].set(largest)


def block_scale(key, extent, pieces, smallest, top_value):
    def one(position, blocks):
        steps = jax.random.uniform(jax.random.fold_in(jax.random.fold_in(key, 6), position), (blocks,), jnp.float32, smallest / len(pieces), top_value / len(pieces))
        return jnp.repeat(jnp.exp(steps), extent[position] // blocks).reshape((-1,) + (1,) * (len(extent) - position - 1))

    gain = one(*pieces[0])
    for cut in pieces[1:]:
        gain = gain * one(*cut)
    return gain


def normal_values(stream_key, shape, spread, bound, pieces=(), held_as=jnp.bfloat16):
    loudness = block_scale(stream_key, shape, pieces, -0.22, 0.18) if pieces else 1.0
    array = jax.random.normal(stream_key, shape, jnp.float32) * spread * loudness
    return jnp.minimum(jnp.maximum(array, -bound), bound).astype(held_as)


def setup_inputs(seed: int = 0) -> dict:
    streams_of = jax.random.split(jax.random.key(seed), 15)
    state = normal_values(streams_of[0], (5, GRIDS, NN, NS), 1.0, 6.0, ((1, 4), (2, 16), (3, 4)), jnp.float32)
    iblank = touch_ends((jax.random.randint(streams_of[1], (GRIDS, NN, NS), 0, 10) < 9).astype(jnp.int32), jax.random.fold_in(streams_of[1], 1), 0, 1)
    flux = normal_values(streams_of[2], (5, 5, GRIDS), 0.5, 3.0, ((2, 4),), jnp.float32)
    left_vectors = draw_left_vectors(jax.random.fold_in(streams_of[14], 71), 0)
    right_vectors = draw_right_vectors(jax.random.fold_in(streams_of[14], 71), 0)
    low_one = draw_low_one(jax.random.fold_in(streams_of[14], 71), 0)
    low_two = draw_low_two(jax.random.fold_in(streams_of[14], 71), 0)
    up_one = draw_up_one(jax.random.fold_in(streams_of[14], 71), 0)
    up_two = draw_up_two(jax.random.fold_in(streams_of[14], 71), 0)
    pivot = draw_pivot(jax.random.fold_in(streams_of[14], 71), 0)
    donor_cells = touch_ends(jax.random.randint(streams_of[10], (8, GRIDS, N_NORMAL * GRIDS * CAP, N_SPAN * BLOCK), 0, CN * CS), jax.random.fold_in(streams_of[10], 1), 0, (CN * CS) - 1).astype(jnp.int32)
    donor_weights = draw_donor_weights(jax.random.fold_in(streams_of[14], 71), 0)
    fringe_cells = draw_fringe_cells(jax.random.fold_in(streams_of[14], 71), 0)
    fringe_live = draw_fringe_live(jax.random.fold_in(streams_of[14], 71), 0)
    return dict(state=state, iblank=iblank, flux=flux, left_vectors=left_vectors, right_vectors=right_vectors, low_one=low_one, low_two=low_two, up_one=up_one, up_two=up_two, pivot=pivot, donor_cells=donor_cells, donor_weights=donor_weights, fringe_cells=fringe_cells, fringe_live=fringe_live)


DISSIP = 0.06
STEP = 0.4
HIGH = lax.Precision.HIGHEST


def to_blocks(values):
    shaped = values.reshape(5, GRIDS, N_NORMAL, CN, N_SPAN, CS)
    return shaped.transpose(1, 2, 4, 0, 3, 5).reshape(GRIDS, N_NORMAL, N_SPAN, 5, CN * CS)


def from_blocks(blocks):
    shaped = blocks.reshape(GRIDS, N_NORMAL, N_SPAN, 5, CN, CS)
    return shaped.transpose(3, 0, 1, 4, 2, 5).reshape(5, GRIDS, N_NORMAL * CN, N_SPAN * CS)


def slot_blocks(slots):
    shaped = slots.reshape(8, GRIDS, N_NORMAL, GRIDS, CAP, N_SPAN, BLOCK)
    return shaped.transpose(1, 2, 5, 0, 3, 4, 6).reshape(GRIDS, N_NORMAL, N_SPAN, 8, GRIDS * CAP * BLOCK)


def fringe_layout(slots):
    shaped = slots.reshape(GRIDS, N_NORMAL, GRIDS, CAP, N_SPAN, BLOCK)
    return shaped.transpose(0, 1, 4, 2, 3, 5).reshape(GRIDS, N_NORMAL, N_SPAN, GRIDS * CAP * BLOCK)


def interpolate(source, corners, weights):
    picked = jnp.take(source, corners, axis=1)
    return jnp.sum(weights[None] * picked, axis=1)


def place(target, values, cells, live):
    existing = jnp.take(target, cells, axis=1)
    return target.at[:, cells].set(jnp.where(live[None] == 1, values, existing))


def overset(state_blocks, donor_blocks, weight_blocks, fringe_blocks, live_blocks):
    def one_source(inputs):
        source, corners, weights = inputs
        return jax.vmap(jax.vmap(interpolate))(source, corners, weights)

    sent = lax.map(one_source, (state_blocks, donor_blocks, weight_blocks))
    sent = sent.reshape(GRIDS, N_NORMAL, N_SPAN, 5, GRIDS, CAP * BLOCK)
    received = sent.transpose(4, 1, 2, 3, 0, 5).reshape(GRIDS, N_NORMAL, N_SPAN, 5, GRIDS * CAP * BLOCK)
    return jax.vmap(jax.vmap(jax.vmap(place)))(state_blocks, received, fringe_blocks, live_blocks)


def residual_of(padded, mixing, form):
    center = padded[..., 2:-2, 2:-2]
    central = padded[..., 2:-2, 3:-1] - padded[..., 2:-2, 1:-3]
    normal_fourth = (padded[..., 4:, 2:-2] - 4.0 * padded[..., 3:-1, 2:-2] + 6.0 * center
                     - 4.0 * padded[..., 1:-3, 2:-2] + padded[..., :-4, 2:-2])
    span_fourth = (padded[..., 2:-2, 4:] - 4.0 * padded[..., 2:-2, 3:-1] + 6.0 * center
                   - 4.0 * padded[..., 2:-2, 1:-3] + padded[..., 2:-2, :-4])
    transported = jnp.einsum(form, mixing, central, precision=HIGH)
    return -0.5 * transported - DISSIP * (normal_fourth + span_fourth)


def line_sweep(values, first, second, reverse):
    def advance(carried, inputs):
        prev_one, prev_two = carried
        value, coef_one, coef_two = inputs
        now = value - coef_one * prev_one - coef_two * prev_two
        return (now, prev_one), now

    empty_part = jnp.zeros((values.shape[0], values.shape[1], values.shape[3]), jnp.float32)
    moved = tuple(jnp.moveaxis(member, 2, 0) for member in (values, first, second))
    _, output = lax.scan(advance, (empty_part, empty_part), moved, reverse=reverse)
    return jnp.moveaxis(output, 0, 2)


def reference(state, iblank, flux, left_vectors, right_vectors, low_one, low_two, up_one, up_two, pivot, donor_cells, donor_weights, fringe_cells, fringe_live):
    donor_blocks = slot_blocks(donor_cells)
    weight_blocks = slot_blocks(donor_weights)
    fringe_blocks = fringe_layout(fringe_cells)
    live_blocks = fringe_layout(fringe_live)
    active = iblank.astype(jnp.float32)[None]
    current = state
    for repeat in range(ITERS):
        current = from_blocks(overset(to_blocks(current), donor_blocks, weight_blocks, fringe_blocks, live_blocks))
        padded = jnp.pad(current, ((0, 0), (0, 0), (2, 2), (2, 2)))
        residual = residual_of(padded, flux, "ckg,kgns->cgns")
        source = STEP * jnp.einsum("ckgs,kgns->cgns", left_vectors, residual, precision=HIGH)
        lower = line_sweep(source, low_one, low_two, False)
        solved = line_sweep(pivot * lower, up_one, up_two, True)
        current = current + active * jnp.einsum("ckgs,kgns->cgns", right_vectors, solved, precision=HIGH)
    return current
```

```python
import jax
import jax.numpy as jnp
from jax import lax
from jax.experimental import pallas as pl
from jax.experimental.pallas import tpu as pltpu
from jax.sharding import PartitionSpec as P

ITERS = 2
GRIDS = 4
SPANS = 4
NORMALS = 16
CAP = 6
ROWS = 16
COMP = 5
LINE = 40
ORDER = (2, 1, 3)
F32, BF16 = jnp.float32, jnp.bfloat16
LANE_GATHER = lax.GatherDimensionNumbers(
    offset_dims=(),
    collapsed_slice_dims=(1,),
    start_index_map=(1,),
    operand_batching_dims=(0,),
    start_indices_batching_dims=(0,),
)


def lane_gather(table, index):
    return lax.gather(
        table,
        index[:, :, None],
        LANE_GATHER,
        slice_sizes=(1, 1),
        mode=lax.GatherScatterMode.PROMISE_IN_BOUNDS,
    )


def iota(shape, dim):
    return lax.broadcasted_iota(jnp.int32, shape, dim)


def to_lines(raw, lines):
    for c in range(COMP):
        for half in range(2):
            for a in range(8):
                tile = raw[c, half * 8 : half * 8 + 8, a * 128 : a * 128 + 128]
                lines[pl.ds(half * 8 * LINE + c * 8 + a, 8, stride=LINE), :] = tile


def kernel(
    state,
    iblank,
    flux,
    left,
    right,
    low_one,
    low_two,
    up_one,
    up_two,
    pivot,
    donor_cells,
    donor_weights,
    fringe_cells,
    fringe_live,
    out,
    raw,
    iblank_v,
    flux_v,
    left_v,
    right_v,
    cells_v,
    weights_v,
    fringe_v,
    live_v,
    cur,
    low1,
    low2,
    up1,
    up2,
    piv,
    active,
    mix_c,
    mix_d,
    src,
    one_rows,
    two_rows,
    table,
    onehots,
    inverse,
    inv_row,
    inv_lane,
    sent,
    received,
    ysend,
    yrecv,
    halo_l,
    halo_r,
    zlo,
    zhi,
    mats,
    mats_in,
    bounds,
    bounds_in,
    enter_out,
    enter,
    in_sem,
    slot_ssem,
    slot_rsem,
    y_ssem,
    y_rsem,
    z_ssem,
    z_rsem,
    mat_ssem,
    mat_rsem,
    b_ssem,
    b_rsem,
    e_ssem,
    e_rsem,
):
    g = lax.axis_index("grid")
    s = lax.axis_index("span")
    n = lax.axis_index("normal")
    leader = jnp.logical_and(lax.rem(n, 3) == 0, n < 15)
    comp_me = lax.div(n, 3)

    pairs = [
        (state, raw.at[0]),
        (donor_cells, cells_v),
        (donor_weights, weights_v),
        (low_one, raw.at[1]),
        (low_two, raw.at[2]),
        (up_one, raw.at[3]),
        (up_two, raw.at[4]),
        (pivot, raw.at[5]),
        (fringe_cells, fringe_v),
        (fringe_live, live_v),
        (left, left_v),
        (flux, flux_v),
        (right, right_v),
        (iblank, iblank_v),
    ]
    loads = [pltpu.make_async_copy(a, b, in_sem.at[k]) for k, (a, b) in enumerate(pairs)]
    for load in loads:
        load.start()

    barrier = pltpu.get_barrier_semaphore()
    for k in range(1, GRIDS):
        pl.semaphore_signal(barrier, inc=1, device_id={"grid": lax.rem(g + k, GRIDS)})
    for k in range(1, NORMALS):
        pl.semaphore_signal(barrier, inc=1, device_id={"normal": lax.rem(n + k, NORMALS)})

    for k in (1, SPANS - 1):
        pl.semaphore_signal(barrier, inc=1, device_id={"span": lax.rem(s + k, SPANS)})

    def barrier_wait():
        pl.semaphore_wait(barrier, GRIDS - 1 + NORMALS - 1 + 2)

    zeros8 = jnp.zeros((8, 128), F32)

    @pl.when(s == 0)
    def _():
        for it in range(ITERS):
            yrecv[it, 0] = zeros8

    @pl.when(s == SPANS - 1)
    def _():
        for it in range(ITERS):
            yrecv[it, 1] = zeros8

    @pl.when(n == 0)
    def _():
        for it in range(ITERS):
            zlo[it] = jnp.zeros((2 * LINE, 128), F32)

    @pl.when(n == NORMALS - 1)
    def _():
        for it in range(ITERS):
            zhi[it] = jnp.zeros((2 * LINE, 128), F32)

    loads[0].wait()
    to_lines(raw.at[0], cur)
    loads[1].wait()
    loads[2].wait()

    def slot_copy(it, k):
        return pltpu.make_async_remote_copy(
            src_ref=sent.at[it, k - 1],
            dst_ref=received.at[it, k - 1],
            send_sem=slot_ssem.at[it, k - 1],
            recv_sem=slot_rsem.at[it, k - 1],
            device_id={"grid": lax.rem(g + k, GRIDS)},
            device_id_type=pl.DeviceIdType.MESH,
        )

    def y_copy(it, side):
        return pltpu.make_async_remote_copy(
            src_ref=ysend.at[it, side],
            dst_ref=yrecv.at[it, side],
            send_sem=y_ssem.at[it, side],
            recv_sem=y_rsem.at[it, side],
            device_id={"span": s + (1 if side == 0 else -1)},
            device_id_type=pl.DeviceIdType.MESH,
        )

    def z_copy(it, side):
        return pltpu.make_async_remote_copy(
            src_ref=cur.at[pl.ds((ROWS - 2) * LINE if side == 0 else 0, 2 * LINE), :],
            dst_ref=(zlo if side == 0 else zhi).at[it],
            send_sem=z_ssem.at[it, side],
            recv_sem=z_rsem.at[it, side],
            device_id={"normal": n + (1 if side == 0 else -1)},
            device_id_type=pl.DeviceIdType.MESH,
        )

    def mat_copy(c):
        return pltpu.make_async_remote_copy(
            src_ref=mats.at[c],
            dst_ref=mats_in.at[n],
            send_sem=mat_ssem.at[c],
            recv_sem=mat_rsem.at[n],
            device_id={"normal": 3 * c},
            device_id_type=pl.DeviceIdType.MESH,
        )

    def b_copy(it, c):
        return pltpu.make_async_remote_copy(
            src_ref=bounds.at[it, c],
            dst_ref=bounds_in.at[it, n],
            send_sem=b_ssem.at[it, c],
            recv_sem=b_rsem.at[it, n],
            device_id={"normal": 3 * c},
            device_id_type=pl.DeviceIdType.MESH,
        )

    def b_arrival(it, k):
        return pltpu.make_async_remote_copy(
            src_ref=bounds.at[it, 0],
            dst_ref=bounds_in.at[it, k],
            send_sem=b_ssem.at[it, 0],
            recv_sem=b_rsem.at[it, k],
            device_id={"normal": k},
            device_id_type=pl.DeviceIdType.MESH,
        )

    def mat_arrival(k):
        return pltpu.make_async_remote_copy(
            src_ref=mats.at[0],
            dst_ref=mats_in.at[k],
            send_sem=mat_ssem.at[0],
            recv_sem=mat_rsem.at[k],
            device_id={"normal": k},
            device_id_type=pl.DeviceIdType.MESH,
        )

    def e_copy(it, k):
        return pltpu.make_async_remote_copy(
            src_ref=enter_out.at[it, k],
            dst_ref=enter.at[it, comp_me],
            send_sem=e_ssem.at[it, k],
            recv_sem=e_rsem.at[it, comp_me],
            device_id={"normal": k},
            device_id_type=pl.DeviceIdType.MESH,
        )

    def e_arrival(it, c):
        return pltpu.make_async_remote_copy(
            src_ref=enter_out.at[it, 0],
            dst_ref=enter.at[it, c],
            send_sem=e_ssem.at[it, 0],
            recv_sem=e_rsem.at[it, c],
            device_id={"normal": 3 * c},
            device_id_type=pl.DeviceIdType.MESH,
        )

    def interpolate(it):
        for c in range(COMP):
            for m in range(0, 8, 2):
                for p in range(2):
                    x = jnp.concatenate(
                        [
                            cur[(2 * m + p) * LINE + c * 8 : (2 * m + p) * LINE + c * 8 + 8, :],
                            cur[(2 * m + 2 + p) * LINE + c * 8 : (2 * m + 2 + p) * LINE + c * 8 + 8, :],
                        ],
                        axis=0,
                    )
                    head = x.astype(BF16)
                    tail = (x - head.astype(F32)).astype(BF16)
                    rows = slice(c * 64 + m * 8, c * 64 + m * 8 + 16)
                    table[rows, p * 128 : p * 128 + 128] = head
                    table[rows, 256 + p * 128 : 256 + p * 128 + 128] = tail
        for turn, k in enumerate(ORDER):
            receiver = lax.rem(g + k, GRIDS)

            def one_row(b, _, k=k, receiver=receiver):
                row = receiver * CAP + b
                total = [zeros8] * COMP
                for pair in range(4):
                    cells = [cells_v[2 * pair + e, pl.ds(row, 1), :] for e in range(2)]
                    if it == 0:
                        parts = []
                        for cell in cells:
                            low = ((cell >> 10) & 1) * 128 + (cell & 127)
                            low = jnp.broadcast_to(low.astype(F32).astype(BF16), (256, 128))
                            rank = iota((256, 128), 0).astype(F32).astype(BF16)
                            parts.append(
                                jnp.where(rank == low, jnp.ones((), BF16), jnp.zeros((), BF16))
                            )
                        hot = jnp.concatenate(parts, axis=1)
                        onehots[((k - 1) * CAP + b) * 4 + pair] = hot
                    else:
                        hot = onehots[((k - 1) * CAP + b) * 4 + pair]
                    found = jnp.dot(
                        table[...],
                        jnp.concatenate([hot, hot], axis=0),
                        preferred_element_type=F32,
                    )
                    for e in range(2):
                        high = ((cells[e] >> 11) << 3) | ((cells[e] >> 7) & 7)
                        weight = jnp.broadcast_to(
                            weights_v[2 * pair + e, pl.ds(row, 1), :], (8, 128)
                        )
                        for v in range(8):
                            mask = jnp.where(iota((8, 128), 0) + v * 8 == high, weight, 0.0)
                            for c in range(COMP):
                                at = c * 64 + v * 8
                                total[c] = (
                                    total[c] + found[at : at + 8, e * 128 : e * 128 + 128] * mask
                                )
                for c in range(COMP):
                    sent[it, k - 1, pl.ds(b * COMP + c, 1), :] = jnp.sum(
                        total[c], axis=0, keepdims=True
                    )
                return 0

            lax.fori_loop(0, CAP, one_row, 0)
            if it == 0 and turn == 0:
                barrier_wait()
            slot_copy(it, k).start()

    def invert_fringe():
        inverse[...] = jnp.zeros((256, 128), F32)
        for k in ORDER:
            source = lax.rem(g + GRIDS - k, GRIDS)

            def one(b, _, k=k, source=source):
                row = source * CAP + b
                cell = fringe_v[pl.ds(row, 1), :]
                live = live_v[pl.ds(row, 1), :]
                high = jnp.where(live == 1, cell >> 7, -1)
                low = cell & 127
                number = (((k - 1) * CAP + b) + 1).astype(F32)
                at = jnp.where(iota((128, 128), 0) == high, 1.0, 0.0)
                lane = iota((128, 128), 1).astype(F32)
                a = jnp.concatenate([at * number, at * lane], axis=0).astype(BF16)
                col = jnp.where(iota((128, 128), 0) == low, 1.0, 0.0).astype(BF16)
                inverse[...] += lax.dot_general(
                    a, col, (((1,), (1,)), ((), ())), preferred_element_type=F32
                )
                return 0

            lax.fori_loop(0, CAP, one, 0)
        inv_row[...] = inverse[0:128, :].astype(jnp.int32) - 1
        inv_lane[...] = inverse[128:256, :].astype(jnp.int32)

    def line(ref, i):
        return ref[i * LINE : i * LINE + LINE, :]

    def block_matrices():
        zero = jnp.zeros((LINE, 128), F32)
        ones = jnp.ones((LINE, 128), F32)
        a1, a2, b1, b2 = ones, zero, zero, ones
        for i in range(ROWS):
            c1, c2 = line(low1, i), line(low2, i)
            a1, a2 = -c1 * a1 - c2 * a2, a1
            b1, b2 = -c1 * b1 - c2 * b2, b1
            one_rows[i * LINE : i * LINE + LINE, :] = a1
            two_rows[i * LINE : i * LINE + LINE, :] = b1
        found = [a1, b1, a2, b2]
        a1, a2, b1, b2 = ones, zero, zero, ones
        p1 = p2 = q1 = q2 = zero
        for i in reversed(range(ROWS)):
            c1, c2, pv = line(up1, i), line(up2, i), line(piv, i)
            a1, a2 = -c1 * a1 - c2 * a2, a1
            b1, b2 = -c1 * b1 - c2 * b2, b1
            p1, p2 = pv * line(one_rows, i) - c1 * p1 - c2 * p2, p1
            q1, q2 = pv * line(two_rows, i) - c1 * q1 - c2 * q2, q1
        found += [a1, b1, a2, b2, p1, q1, p2, q2]
        for c in range(COMP):
            for j, whole in enumerate(found):
                mats[c, j] = whole[c * 8 : c * 8 + 8, :]

    def prepare():
        for k, lines in ((3, low1), (4, low2), (5, up1), (6, up2), (7, piv)):
            loads[k].wait()
            to_lines(raw.at[k - 2], lines)
        block_matrices()
        for c in range(COMP):

            @pl.when(n != 3 * c)
            def _(c=c):
                mat_copy(c).start()

        @pl.when(leader)
        def _():
            mats_in[n] = mats[comp_me]

        loads[8].wait()
        loads[9].wait()
        invert_fringe()

    def prepare_mixing():
        loads[10].wait()
        loads[11].wait()
        f = [[jnp.broadcast_to(flux_v[k, m : m + 1].reshape(1, 1), (8, 128)) for m in range(COMP)] for k in range(COMP)]
        for c in range(COMP):
            row = [left_v[c * COMP + k] for k in range(COMP)]
            for m in range(COMP):
                total = row[0] * f[0][m]
                for k in range(1, COMP):
                    total = total + row[k] * f[k][m]
                mix_c[c * COMP + m] = total * -0.2
                mix_d[c * COMP + m] = row[m] * -0.024

    def place_rows(it, k, i_list):
        for i in i_list:
            lanes = inv_lane[i * 8 : i * 8 + 8, :]
            rows = inv_row[i * 8 : i * 8 + 8, :]
            values = [cur[i * LINE + c * 8 : i * LINE + c * 8 + 8, :] for c in range(COMP)]
            for b in range(CAP):
                hit = rows == (k - 1) * CAP + b
                for c in range(COMP):
                    slots = received[it, k - 1, pl.ds(b * COMP + c, 8, stride=0), :]
                    values[c] = jnp.where(hit, lane_gather(slots, lanes), values[c])
            for c in range(COMP):
                cur[i * LINE + c * 8 : i * LINE + c * 8 + 8, :] = values[c]

    def place(it):
        for turn, k in enumerate(ORDER):
            slot_copy(it, k).wait_recv()
            if turn == GRIDS - 2:
                place_rows(it, k, (0, 1, 14, 15))
                start_z(it)
                place_rows(it, k, range(2, 14))
            else:
                place_rows(it, k, range(ROWS))

    def start_z(it):
        @pl.when(n < NORMALS - 1)
        def _():
            z_copy(it, 0).start()

        @pl.when(n > 0)
        def _():
            z_copy(it, 1).start()

    def start_y(it):
        lane = iota((8, 128), 1)
        for side in range(2):
            total = zeros8
            for m in range(10):
                rows = cur[pl.ds(m * 64 + (7 if side == 0 else 0), 8, stride=8), :]
                shift = (2 * m + (2 if side == 0 else 0)) % 128
                rows = pltpu.roll(rows, shift, 1) if shift else rows
                total = jnp.where((lane >> 1) == m, rows, total)
            ysend[it, side] = total

        @pl.when(s < SPANS - 1)
        def _():
            y_copy(it, 0).start()

        @pl.when(s > 0)
        def _():
            y_copy(it, 1).start()

    def finish_y(it):
        @pl.when(s > 0)
        def _():
            y_copy(it, 0).wait_recv()

        @pl.when(s < SPANS - 1)
        def _():
            y_copy(it, 1).wait_recv()

        for side, halo in ((0, halo_l), (1, halo_r)):
            packed = yrecv[it, side]
            for m in range(10):
                shift = (126 - 2 * m) if side == 0 else (128 - 2 * m) % 128
                halo[m * 8 : m * 8 + 8, :] = pltpu.roll(packed, shift, 1) if shift else packed

    def source_row(it, i):
        lane = iota((8, 128), 1)
        sub = iota((8, 128), 0)

        def at(row, c):
            if row < 0:
                return zlo[it, (row + 2) * LINE + c * 8 : (row + 2) * LINE + c * 8 + 8, :]
            if row >= ROWS:
                return zhi[it, (row - ROWS) * LINE + c * 8 : (row - ROWS) * LINE + c * 8 + 8, :]
            return cur[row * LINE + c * 8 : row * LINE + c * 8 + 8, :]

        central, fourth = [], []
        for c in range(COMP):
            x = at(i, c)
            above = jnp.where(
                sub == 7, halo_r[pl.ds(i * COMP + c, 8, stride=0), :], pltpu.roll(x, 7, 0)
            )
            below = jnp.where(
                sub == 0, halo_l[pl.ds(i * COMP + c, 8, stride=0), :], pltpu.roll(x, 1, 0)
            )
            plus1 = pltpu.roll(jnp.where(lane < 1, above, x), 127, 1)
            plus2 = pltpu.roll(jnp.where(lane < 2, above, x), 126, 1)
            minus1 = pltpu.roll(jnp.where(lane >= 127, below, x), 1, 1)
            minus2 = pltpu.roll(jnp.where(lane >= 126, below, x), 2, 1)
            central.append(plus1 - minus1)
            near = (plus1 + minus1) + (at(i + 1, c) + at(i - 1, c))
            far = (plus2 + minus2) + (at(i + 2, c) + at(i - 2, c))
            fourth.append(far - 4.0 * near + 12.0 * x)
        for c in range(COMP):
            total = mix_c[c * COMP] * central[0] + mix_d[c * COMP] * fourth[0]
            for m in range(1, COMP):
                total = total + mix_c[c * COMP + m] * central[m] + mix_d[c * COMP + m] * fourth[m]
            src[i * LINE + c * 8 : i * LINE + c * 8 + 8, :] = total

    def sweep(e1, e2, f1, f2):
        for i in range(ROWS):
            e1, e2 = line(src, i) - line(low1, i) * e1 - line(low2, i) * e2, e1
            one_rows[i * LINE : i * LINE + LINE, :] = e1
        for i in reversed(range(ROWS)):
            f1, f2 = line(piv, i) * line(one_rows, i) - line(up1, i) * f1 - line(up2, i) * f2, f1
            two_rows[i * LINE : i * LINE + LINE, :] = f1
        return e1, e2, f1, f2

    def lead(it):
        def arrive(k, _):
            @pl.when(k != n)
            def _():
                if it == 0:
                    mat_arrival(k).wait_recv()
                b_arrival(it, k).wait_recv()

            return 0

        lax.fori_loop(0, NORMALS, arrive, 0)
        e1 = e2 = zeros8
        pushed = []
        for k in range(NORMALS):
            enter_out[it, k, 0] = e1
            enter_out[it, k, 1] = e2
            pushed.append(
                (
                    mats_in[k, 8] * e1 + mats_in[k, 9] * e2 + bounds_in[it, k, 2],
                    mats_in[k, 10] * e1 + mats_in[k, 11] * e2 + bounds_in[it, k, 3],
                )
            )
            e1, e2 = (
                mats_in[k, 0] * e1 + mats_in[k, 1] * e2 + bounds_in[it, k, 0],
                mats_in[k, 2] * e1 + mats_in[k, 3] * e2 + bounds_in[it, k, 1],
            )
        f1 = f2 = zeros8
        for k in reversed(range(NORMALS)):
            enter_out[it, k, 2] = f1
            enter_out[it, k, 3] = f2
            f1, f2 = (
                mats_in[k, 4] * f1 + mats_in[k, 5] * f2 + pushed[k][0],
                mats_in[k, 6] * f1 + mats_in[k, 7] * f2 + pushed[k][1],
            )
        for far in range(8, 0, -1):
            for off in {far, NORMALS - far}:
                e_copy(it, lax.rem(n + off, NORMALS)).start()
        enter[it, comp_me] = enter_out[it, n]

    def lines_step(it):
        zero = jnp.zeros((LINE, 128), F32)
        found = sweep(zero, zero, zero, zero)
        for c in range(COMP):
            for j, whole in enumerate(found):
                bounds[it, c, j] = whole[c * 8 : c * 8 + 8, :]
        for c in range(COMP):

            @pl.when(n != 3 * c)
            def _(c=c):
                b_copy(it, c).start()

        @pl.when(leader)
        def _():
            bounds_in[it, n] = bounds[it, comp_me]
            lead(it)

        if it == 0:
            finish_loads()
        for c in range(COMP):

            @pl.when(n != 3 * c)
            def _(c=c):
                e_arrival(it, c).wait_recv()

        entering = [
            jnp.concatenate([enter[it, c, j] for c in range(COMP)], axis=0) for j in range(4)
        ]
        sweep(*entering)

    def finish_loads():
        loads[12].wait()
        loads[13].wait()
        for half in range(2):
            for a in range(8):
                tile = iblank_v[half * 8 : half * 8 + 8, a * 128 : a * 128 + 128]
                active[pl.ds(half * 64 + a, 8, stride=8), :] = tile.astype(F32)

    def update(it):
        for i in range(ROWS):
            solved = [two_rows[i * LINE + m * 8 : i * LINE + m * 8 + 8, :] for m in range(COMP)]
            mask = active[i * 8 : i * 8 + 8, :]
            for c in range(COMP):
                total = right_v[c * COMP] * solved[0]
                for m in range(1, COMP):
                    total = total + right_v[c * COMP + m] * solved[m]
                at = slice(i * LINE + c * 8, i * LINE + c * 8 + 8)
                cur[at, :] = cur[at, :] + mask * total

    for it in range(ITERS):
        interpolate(it)
        if it == 0:
            prepare()
            prepare_mixing()
        place(it)
        start_y(it)
        finish_y(it)
        for i in range(2, ROWS - 2):
            source_row(it, i)

        @pl.when(n > 0)
        def _(it=it):
            z_copy(it, 0).wait_recv()

        @pl.when(n < NORMALS - 1)
        def _(it=it):
            z_copy(it, 1).wait_recv()

        for i in (0, 1, ROWS - 2, ROWS - 1):
            source_row(it, i)
        lines_step(it)

        @pl.when(n < NORMALS - 1)
        def _(it=it):
            z_copy(it, 0).wait_send()

        @pl.when(n > 0)
        def _(it=it):
            z_copy(it, 1).wait_send()

        update(it)

    for c in range(COMP):
        for half in range(2):
            for a in range(8):
                out[c, half * 8 : half * 8 + 8, a * 128 : a * 128 + 128] = cur[
                    pl.ds(half * 8 * LINE + c * 8 + a, 8, stride=LINE), :
                ]

    for it in range(ITERS):
        for k in ORDER:
            slot_copy(it, k).wait_send()

        @pl.when(s < SPANS - 1)
        def _(it=it):
            y_copy(it, 0).wait_send()

        @pl.when(s > 0)
        def _(it=it):
            y_copy(it, 1).wait_send()

        for c in range(COMP):

            @pl.when(n != 3 * c)
            def _(c=c, it=it):
                if it == 0:
                    mat_copy(c).wait_send()
                b_copy(it, c).wait_send()

        @pl.when(leader)
        def _(it=it):
            for off in range(1, NORMALS):
                e_copy(it, lax.rem(n + off, NORMALS)).wait_send()


def vmem(*shape, dtype=F32):
    return pltpu.VMEM(shape, dtype)


def local(
    state,
    iblank,
    flux,
    left_vectors,
    right_vectors,
    low_one,
    low_two,
    up_one,
    up_two,
    pivot,
    donor_cells,
    donor_weights,
    fringe_cells,
    fringe_live,
):
    dma = pltpu.SemaphoreType.DMA
    whole = ROWS * LINE
    slots = GRIDS * CAP
    out = pl.pallas_call(
        kernel,
        out_shape=jax.ShapeDtypeStruct((COMP, ROWS, 1024), F32),
        in_specs=[pl.BlockSpec(memory_space=pltpu.HBM)] * 14,
        out_specs=pl.BlockSpec(memory_space=pltpu.VMEM),
        scratch_shapes=[
            vmem(6, COMP, ROWS, 1024),
            vmem(ROWS, 1024, dtype=jnp.int32),
            vmem(COMP, COMP),
            vmem(25, 8, 128),
            vmem(25, 8, 128),
            vmem(8, slots, 128, dtype=jnp.int32),
            vmem(8, slots, 128),
            vmem(slots, 128, dtype=jnp.int32),
            vmem(slots, 128, dtype=jnp.int32),
            vmem(whole, 128),
            vmem(whole, 128),
            vmem(whole, 128),
            vmem(whole, 128),
            vmem(whole, 128),
            vmem(whole, 128),
            vmem(ROWS * 8, 128),
            vmem(25, 8, 128),
            vmem(25, 8, 128),
            vmem(whole, 128),
            vmem(whole, 128),
            vmem(whole, 128),
            vmem(320, 512, dtype=BF16),
            vmem(72, 256, 256, dtype=BF16),
            vmem(256, 128),
            vmem(128, 128, dtype=jnp.int32),
            vmem(128, 128, dtype=jnp.int32),
            vmem(ITERS, 3, CAP * COMP, 128),
            vmem(ITERS, 3, CAP * COMP, 128),
            vmem(ITERS, 2, 8, 128),
            vmem(ITERS, 2, 8, 128),
            vmem(80, 128),
            vmem(80, 128),
            vmem(ITERS, 2 * LINE, 128),
            vmem(ITERS, 2 * LINE, 128),
            vmem(COMP, 12, 8, 128),
            vmem(NORMALS, 12, 8, 128),
            vmem(ITERS, COMP, 4, 8, 128),
            vmem(ITERS, NORMALS, 4, 8, 128),
            vmem(ITERS, NORMALS, 4, 8, 128),
            vmem(ITERS, COMP, 4, 8, 128),
            dma((14,)),
            dma((ITERS, 3)),
            dma((ITERS, 3)),
            dma((ITERS, 2)),
            dma((ITERS, 2)),
            dma((ITERS, 2)),
            dma((ITERS, 2)),
            dma((COMP,)),
            dma((NORMALS,)),
            dma((ITERS, COMP)),
            dma((ITERS, NORMALS)),
            dma((ITERS, NORMALS)),
            dma((ITERS, COMP)),
        ],
        compiler_params=pltpu.CompilerParams(
            collective_id=0, has_side_effects=True, vmem_limit_bytes=48 << 20
        ),
        name="adi_window",
    )(
        state[:, 0],
        iblank[0],
        flux[:, :, 0],
        left_vectors.reshape(25, 8, 128),
        right_vectors.reshape(25, 8, 128),
        low_one[:, 0],
        low_two[:, 0],
        up_one[:, 0],
        up_two[:, 0],
        pivot[:, 0],
        donor_cells[:, 0],
        donor_weights[:, 0],
        fringe_cells[0],
        fringe_live[0],
    )
    return out[:, None]


def solution(mesh):
    cells = P(None, "grid", "normal", "span")
    slots = P("grid", "normal", "span")
    lines = P(None, None, "grid", "span")
    return jax.shard_map(
        local,
        mesh=mesh,
        in_specs=(
            cells,
            slots,
            P(None, None, "grid"),
            lines,
            lines,
            cells,
            cells,
            cells,
            cells,
            cells,
            cells,
            cells,
            slots,
            slots,
        ),
        out_specs=cells,
        check_vma=False,
    )
```

```python
import jax
import jax.numpy as jnp
from jax import lax
from jax.experimental import pallas as pl
from jax.experimental.pallas import tpu as pltpu
from jax.sharding import PartitionSpec as P

ITERS = 2
GRIDS = 4
SPANS = 4
NORMALS = 16
CAP = 6
SLOT_ROWS = GRIDS * CAP
ROWS = 16
COMP = 5
LINE = 40
ORDER = (2, 1, 3)
F32, BF16 = jnp.float32, jnp.bfloat16
LANE_GATHER = lax.GatherDimensionNumbers(
    offset_dims=(),
    collapsed_slice_dims=(1,),
    start_index_map=(1,),
    operand_batching_dims=(0,),
    start_indices_batching_dims=(0,),
)


def lane_gather(table, index):
    return lax.gather(
        table,
        index[:, :, None],
        LANE_GATHER,
        slice_sizes=(1, 1),
        mode=lax.GatherScatterMode.PROMISE_IN_BOUNDS,
    )


def iota(shape, dim):
    return lax.broadcasted_iota(jnp.int32, shape, dim)


def to_lines(raw, lines):
    for c in range(COMP):
        for half in range(2):
            for a in range(8):
                tile = raw[c, half * 8 : half * 8 + 8, a * 128 : a * 128 + 128]
                lines[pl.ds(half * 8 * LINE + c * 8 + a, 8, stride=LINE), :] = tile


def kernel(
    state,
    iblank,
    flux,
    left,
    right,
    low_one,
    low_two,
    up_one,
    up_two,
    pivot,
    donor_cells,
    donor_weights,
    fringe_cells,
    fringe_live,
    out,
    raw,
    iblank_v,
    flux_v,
    left_v,
    right_v,
    cells_v,
    weights_v,
    fringe_v,
    live_v,
    cur,
    low1,
    low2,
    up1,
    up2,
    piv,
    active,
    mix_c,
    mix_d,
    src,
    one_rows,
    two_rows,
    table,
    inverse,
    inv_row,
    inv_lane,
    sent,
    received,
    ysend,
    yrecv,
    halo_l,
    halo_r,
    zlo,
    zhi,
    mats,
    mats_in,
    bounds,
    bounds_in,
    enter_out,
    enter,
    in_sem,
    slot_ssem,
    slot_rsem,
    y_ssem,
    y_rsem,
    z_ssem,
    z_rsem,
    mat_ssem,
    mat_rsem,
    b_ssem,
    b_rsem,
    e_ssem,
    e_rsem,
):
    g = lax.axis_index("grid")
    s = lax.axis_index("span")
    n = lax.axis_index("normal")
    leader = jnp.logical_and(lax.rem(n, 3) == 0, n < 15)
    comp_me = lax.div(n, 3)

    pairs = [
        (state, raw.at[0]),
        (donor_cells, cells_v),
        (donor_weights, weights_v),
        (low_one, raw.at[1]),
        (low_two, raw.at[2]),
        (up_one, raw.at[3]),
        (up_two, raw.at[4]),
        (pivot, raw.at[5]),
        (fringe_cells, fringe_v),
        (fringe_live, live_v),
        (left, left_v),
        (flux, flux_v),
        (right, right_v),
        (iblank, iblank_v),
    ]
    loads = [pltpu.make_async_copy(a, b, in_sem.at[k]) for k, (a, b) in enumerate(pairs)]
    for load in loads:
        load.start()

    barrier = pltpu.get_barrier_semaphore()
    for k in range(1, GRIDS):
        pl.semaphore_signal(barrier, inc=1, device_id={"grid": lax.rem(g + k, GRIDS)})
    for k in range(1, NORMALS):
        pl.semaphore_signal(barrier, inc=1, device_id={"normal": lax.rem(n + k, NORMALS)})

    for k in (1, SPANS - 1):
        pl.semaphore_signal(barrier, inc=1, device_id={"span": lax.rem(s + k, SPANS)})

    def barrier_wait():
        pl.semaphore_wait(barrier, GRIDS - 1 + NORMALS - 1 + 2)

    zeros8 = jnp.zeros((8, 128), F32)

    @pl.when(s == 0)
    def _():
        for it in range(ITERS):
            yrecv[it, 0] = zeros8

    @pl.when(s == SPANS - 1)
    def _():
        for it in range(ITERS):
            yrecv[it, 1] = zeros8

    @pl.when(n == 0)
    def _():
        for it in range(ITERS):
            zlo[it] = jnp.zeros((2 * LINE, 128), F32)

    @pl.when(n == NORMALS - 1)
    def _():
        for it in range(ITERS):
            zhi[it] = jnp.zeros((2 * LINE, 128), F32)

    loads[0].wait()
    to_lines(raw.at[0], cur)
    loads[1].wait()
    loads[2].wait()

    def slot_copy(it, k):
        return pltpu.make_async_remote_copy(
            src_ref=sent.at[it, k - 1],
            dst_ref=received.at[it, k - 1],
            send_sem=slot_ssem.at[it, k - 1],
            recv_sem=slot_rsem.at[it, k - 1],
            device_id={"grid": lax.rem(g + k, GRIDS)},
            device_id_type=pl.DeviceIdType.MESH,
        )

    def y_copy(it, side):
        return pltpu.make_async_remote_copy(
            src_ref=ysend.at[it, side],
            dst_ref=yrecv.at[it, side],
            send_sem=y_ssem.at[it, side],
            recv_sem=y_rsem.at[it, side],
            device_id={"span": s + (1 if side == 0 else -1)},
            device_id_type=pl.DeviceIdType.MESH,
        )

    def z_copy(it, side):
        return pltpu.make_async_remote_copy(
            src_ref=cur.at[pl.ds((ROWS - 2) * LINE if side == 0 else 0, 2 * LINE), :],
            dst_ref=(zlo if side == 0 else zhi).at[it],
            send_sem=z_ssem.at[it, side],
            recv_sem=z_rsem.at[it, side],
            device_id={"normal": n + (1 if side == 0 else -1)},
            device_id_type=pl.DeviceIdType.MESH,
        )

    def mat_copy(c):
        return pltpu.make_async_remote_copy(
            src_ref=mats.at[c],
            dst_ref=mats_in.at[n],
            send_sem=mat_ssem.at[c],
            recv_sem=mat_rsem.at[n],
            device_id={"normal": 3 * c},
            device_id_type=pl.DeviceIdType.MESH,
        )

    def b_copy(it, c):
        return pltpu.make_async_remote_copy(
            src_ref=bounds.at[it, c],
            dst_ref=bounds_in.at[it, n],
            send_sem=b_ssem.at[it, c],
            recv_sem=b_rsem.at[it, n],
            device_id={"normal": 3 * c},
            device_id_type=pl.DeviceIdType.MESH,
        )

    def b_arrival(it, k):
        return pltpu.make_async_remote_copy(
            src_ref=bounds.at[it, 0],
            dst_ref=bounds_in.at[it, k],
            send_sem=b_ssem.at[it, 0],
            recv_sem=b_rsem.at[it, k],
            device_id={"normal": k},
            device_id_type=pl.DeviceIdType.MESH,
        )

    def mat_arrival(k):
        return pltpu.make_async_remote_copy(
            src_ref=mats.at[0],
            dst_ref=mats_in.at[k],
            send_sem=mat_ssem.at[0],
            recv_sem=mat_rsem.at[k],
            device_id={"normal": k},
            device_id_type=pl.DeviceIdType.MESH,
        )

    def e_copy(it, k):
        return pltpu.make_async_remote_copy(
            src_ref=enter_out.at[it, k],
            dst_ref=enter.at[it, comp_me],
            send_sem=e_ssem.at[it, k],
            recv_sem=e_rsem.at[it, comp_me],
            device_id={"normal": k},
            device_id_type=pl.DeviceIdType.MESH,
        )

    def e_arrival(it, c):
        return pltpu.make_async_remote_copy(
            src_ref=enter_out.at[it, 0],
            dst_ref=enter.at[it, c],
            send_sem=e_ssem.at[it, 0],
            recv_sem=e_rsem.at[it, c],
            device_id={"normal": 3 * c},
            device_id_type=pl.DeviceIdType.MESH,
        )

    def one_hot_pair(row, pair, total):
        cells = [cells_v[pl.ds((2 * pair + e) * SLOT_ROWS + row, 1), :] for e in range(2)]
        parts = []
        for cell in cells:
            low = ((cell >> 10) & 1) * 128 + (cell & 127)
            low = jnp.broadcast_to(low.astype(F32).astype(BF16), (256, 128))
            rank = iota((256, 128), 0).astype(F32).astype(BF16)
            parts.append(jnp.where(rank == low, jnp.ones((), BF16), jnp.zeros((), BF16)))
        hot = jnp.concatenate(parts, axis=1)
        found = jnp.dot(
            table[...], jnp.concatenate([hot, hot], axis=0), preferred_element_type=F32
        )
        for e in range(2):
            high = ((cells[e] >> 11) << 3) | ((cells[e] >> 7) & 7)
            weight = jnp.broadcast_to(
                weights_v[pl.ds((2 * pair + e) * SLOT_ROWS + row, 1), :], (8, 128)
            )
            for v in range(8):
                mask = jnp.where(iota((8, 128), 0) + v * 8 == high, weight, 0.0)
                for c in range(COMP):
                    at = c * 64 + v * 8
                    total[c] = total[c] + found[at : at + 8, e * 128 : e * 128 + 128] * mask

    def interpolate(it):
        for c in range(COMP):
            for m in range(0, 8, 2):
                for p in range(2):
                    x = jnp.concatenate(
                        [
                            cur[(2 * m + p) * LINE + c * 8 : (2 * m + p) * LINE + c * 8 + 8, :],
                            cur[(2 * m + 2 + p) * LINE + c * 8 : (2 * m + 2 + p) * LINE + c * 8 + 8, :],
                        ],
                        axis=0,
                    )
                    head = x.astype(BF16)
                    tail = (x - head.astype(F32)).astype(BF16)
                    rows = slice(c * 64 + m * 8, c * 64 + m * 8 + 16)
                    table[rows, p * 128 : p * 128 + 128] = head
                    table[rows, 256 + p * 128 : 256 + p * 128 + 128] = tail
        for turn, k in enumerate(ORDER):
            receiver = lax.rem(g + k, GRIDS)

            def three_rows(trip, _, k=k, receiver=receiver):
                first = receiver * CAP + 3 * trip
                cells = cells_v[pl.ds(first + 2, 8, stride=SLOT_ROWS), :]
                lanes, blocks = cells & 127, cells >> 7
                picked = [zeros8] * COMP
                sums = [[zeros8] * COMP for _ in range(2)]
                for step in range(8):
                    one_hot_pair(first + step // 4, step % 4, sums[step // 4])
                    for block in range(16 * step, 16 * step + 16):
                        hit = blocks == block
                        at = (block // 8) * LINE + block % 8
                        for c in range(COMP):
                            values = cur[pl.ds(at + c * 8, 8, stride=0), :]
                            picked[c] = jnp.where(hit, lane_gather(values, lanes), picked[c])
                weight = weights_v[pl.ds(first + 2, 8, stride=SLOT_ROWS), :]
                sums.append([p * weight for p in picked])
                for e in range(3):
                    for c in range(COMP):
                        sent[it, k - 1, pl.ds((3 * trip + e) * COMP + c, 1), :] = jnp.sum(
                            sums[e][c], axis=0, keepdims=True
                        )
                return 0

            lax.fori_loop(0, CAP // 3, three_rows, 0)
            if it == 0 and turn == 0:
                barrier_wait()
            slot_copy(it, k).start()

    def invert_fringe():
        inverse[...] = jnp.zeros((256, 128), F32)
        for k in ORDER:
            source = lax.rem(g + GRIDS - k, GRIDS)

            def one(b, _, k=k, source=source):
                row = source * CAP + b
                cell = fringe_v[pl.ds(row, 1), :]
                live = live_v[pl.ds(row, 1), :]
                high = jnp.where(live == 1, cell >> 7, -1)
                low = cell & 127
                number = (((k - 1) * CAP + b) + 1).astype(F32)
                at = jnp.where(iota((128, 128), 0) == high, 1.0, 0.0)
                lane = iota((128, 128), 1).astype(F32)
                a = jnp.concatenate([at * number, at * lane], axis=0).astype(BF16)
                col = jnp.where(iota((128, 128), 0) == low, 1.0, 0.0).astype(BF16)
                inverse[...] += lax.dot_general(
                    a, col, (((1,), (1,)), ((), ())), preferred_element_type=F32
                )
                return 0

            lax.fori_loop(0, CAP, one, 0)
        inv_row[...] = inverse[0:128, :].astype(jnp.int32) - 1
        inv_lane[...] = inverse[128:256, :].astype(jnp.int32)

    def line(ref, i):
        return ref[i * LINE : i * LINE + LINE, :]

    def block_matrices():
        zero = jnp.zeros((LINE, 128), F32)
        ones = jnp.ones((LINE, 128), F32)
        a1, a2, b1, b2 = ones, zero, zero, ones
        for i in range(ROWS):
            c1, c2 = line(low1, i), line(low2, i)
            a1, a2 = -c1 * a1 - c2 * a2, a1
            b1, b2 = -c1 * b1 - c2 * b2, b1
            one_rows[i * LINE : i * LINE + LINE, :] = a1
            two_rows[i * LINE : i * LINE + LINE, :] = b1
        found = [a1, b1, a2, b2]
        a1, a2, b1, b2 = ones, zero, zero, ones
        p1 = p2 = q1 = q2 = zero
        for i in reversed(range(ROWS)):
            c1, c2, pv = line(up1, i), line(up2, i), line(piv, i)
            a1, a2 = -c1 * a1 - c2 * a2, a1
            b1, b2 = -c1 * b1 - c2 * b2, b1
            p1, p2 = pv * line(one_rows, i) - c1 * p1 - c2 * p2, p1
            q1, q2 = pv * line(two_rows, i) - c1 * q1 - c2 * q2, q1
        found += [a1, b1, a2, b2, p1, q1, p2, q2]
        for c in range(COMP):
            for j, whole in enumerate(found):
                mats[c, j] = whole[c * 8 : c * 8 + 8, :]

    def prepare():
        for k, lines in ((3, low1), (4, low2), (5, up1), (6, up2), (7, piv)):
            loads[k].wait()
            to_lines(raw.at[k - 2], lines)
        block_matrices()
        for c in range(COMP):

            @pl.when(n != 3 * c)
            def _(c=c):
                mat_copy(c).start()

        @pl.when(leader)
        def _():
            mats_in[n] = mats[comp_me]

        loads[8].wait()
        loads[9].wait()
        invert_fringe()

    def prepare_mixing():
        loads[10].wait()
        loads[11].wait()
        f = [[jnp.broadcast_to(flux_v[k, :, m : m + 1], (8, 128)) for m in range(COMP)] for k in range(COMP)]
        for c in range(COMP):
            row = [left_v[c * COMP + k] for k in range(COMP)]
            for m in range(COMP):
                total = row[0] * f[0][m]
                for k in range(1, COMP):
                    total = total + row[k] * f[k][m]
                mix_c[c * COMP + m] = total * -0.2
                mix_d[c * COMP + m] = row[m] * -0.024

    def place_rows(it, k, i_list):
        for i in i_list:
            lanes = inv_lane[i * 8 : i * 8 + 8, :]
            rows = inv_row[i * 8 : i * 8 + 8, :]
            values = [cur[i * LINE + c * 8 : i * LINE + c * 8 + 8, :] for c in range(COMP)]
            for b in range(CAP):
                hit = rows == (k - 1) * CAP + b
                for c in range(COMP):
                    slots = received[it, k - 1, pl.ds(b * COMP + c, 8, stride=0), :]
                    values[c] = jnp.where(hit, lane_gather(slots, lanes), values[c])
            for c in range(COMP):
                cur[i * LINE + c * 8 : i * LINE + c * 8 + 8, :] = values[c]

    def place(it):
        for turn, k in enumerate(ORDER):
            slot_copy(it, k).wait_recv()
            if turn == GRIDS - 2:
                place_rows(it, k, (0, 1, 14, 15))
                start_z(it)
                place_rows(it, k, range(2, 14))
            else:
                place_rows(it, k, range(ROWS))

    def start_z(it):
        @pl.when(n < NORMALS - 1)
        def _():
            z_copy(it, 0).start()

        @pl.when(n > 0)
        def _():
            z_copy(it, 1).start()

    def start_y(it):
        lane = iota((8, 128), 1)
        for side in range(2):
            total = zeros8
            for m in range(10):
                rows = cur[pl.ds(m * 64 + (7 if side == 0 else 0), 8, stride=8), :]
                shift = (2 * m + (2 if side == 0 else 0)) % 128
                rows = pltpu.roll(rows, shift, 1) if shift else rows
                total = jnp.where((lane >> 1) == m, rows, total)
            ysend[it, side] = total

        @pl.when(s < SPANS - 1)
        def _():
            y_copy(it, 0).start()

        @pl.when(s > 0)
        def _():
            y_copy(it, 1).start()

    def finish_y(it):
        @pl.when(s > 0)
        def _():
            y_copy(it, 0).wait_recv()

        @pl.when(s < SPANS - 1)
        def _():
            y_copy(it, 1).wait_recv()

        for side, halo in ((0, halo_l), (1, halo_r)):
            packed = yrecv[it, side]
            for m in range(10):
                shift = (126 - 2 * m) if side == 0 else (128 - 2 * m) % 128
                halo[m * 8 : m * 8 + 8, :] = pltpu.roll(packed, shift, 1) if shift else packed

    def source_row(it, i):
        lane = iota((8, 128), 1)
        sub = iota((8, 128), 0)

        def at(row, c):
            if row < 0:
                return zlo[it, (row + 2) * LINE + c * 8 : (row + 2) * LINE + c * 8 + 8, :]
            if row >= ROWS:
                return zhi[it, (row - ROWS) * LINE + c * 8 : (row - ROWS) * LINE + c * 8 + 8, :]
            return cur[row * LINE + c * 8 : row * LINE + c * 8 + 8, :]

        central, fourth = [], []
        for c in range(COMP):
            x = at(i, c)
            above = jnp.where(
                sub == 7, halo_r[pl.ds(i * COMP + c, 8, stride=0), :], pltpu.roll(x, 7, 0)
            )
            below = jnp.where(
                sub == 0, halo_l[pl.ds(i * COMP + c, 8, stride=0), :], pltpu.roll(x, 1, 0)
            )
            plus1 = pltpu.roll(jnp.where(lane < 1, above, x), 127, 1)
            plus2 = pltpu.roll(jnp.where(lane < 2, above, x), 126, 1)
            minus1 = pltpu.roll(jnp.where(lane >= 127, below, x), 1, 1)
            minus2 = pltpu.roll(jnp.where(lane >= 126, below, x), 2, 1)
            central.append(plus1 - minus1)
            near = (plus1 + minus1) + (at(i + 1, c) + at(i - 1, c))
            far = (plus2 + minus2) + (at(i + 2, c) + at(i - 2, c))
            fourth.append(far - 4.0 * near + 12.0 * x)
        for c in range(COMP):
            total = mix_c[c * COMP] * central[0] + mix_d[c * COMP] * fourth[0]
            for m in range(1, COMP):
                total = total + mix_c[c * COMP + m] * central[m] + mix_d[c * COMP + m] * fourth[m]
            src[i * LINE + c * 8 : i * LINE + c * 8 + 8, :] = total

    def sweep(e1, e2, f1, f2):
        for i in range(ROWS):
            e1, e2 = line(src, i) - line(low1, i) * e1 - line(low2, i) * e2, e1
            one_rows[i * LINE : i * LINE + LINE, :] = e1
        for i in reversed(range(ROWS)):
            f1, f2 = line(piv, i) * line(one_rows, i) - line(up1, i) * f1 - line(up2, i) * f2, f1
            two_rows[i * LINE : i * LINE + LINE, :] = f1
        return e1, e2, f1, f2

    def lead(it):
        def arrive(k, _):
            @pl.when(k != n)
            def _():
                if it == 0:
                    mat_arrival(k).wait_recv()
                b_arrival(it, k).wait_recv()

            return 0

        lax.fori_loop(0, NORMALS, arrive, 0)
        e1 = e2 = zeros8
        pushed = []
        for k in range(NORMALS):
            enter_out[it, k, 0] = e1
            enter_out[it, k, 1] = e2
            pushed.append(
                (
                    mats_in[k, 8] * e1 + mats_in[k, 9] * e2 + bounds_in[it, k, 2],
                    mats_in[k, 10] * e1 + mats_in[k, 11] * e2 + bounds_in[it, k, 3],
                )
            )
            e1, e2 = (
                mats_in[k, 0] * e1 + mats_in[k, 1] * e2 + bounds_in[it, k, 0],
                mats_in[k, 2] * e1 + mats_in[k, 3] * e2 + bounds_in[it, k, 1],
            )
        f1 = f2 = zeros8
        for k in reversed(range(NORMALS)):
            enter_out[it, k, 2] = f1
            enter_out[it, k, 3] = f2
            f1, f2 = (
                mats_in[k, 4] * f1 + mats_in[k, 5] * f2 + pushed[k][0],
                mats_in[k, 6] * f1 + mats_in[k, 7] * f2 + pushed[k][1],
            )
        for far in range(8, 0, -1):
            for off in {far, NORMALS - far}:
                e_copy(it, lax.rem(n + off, NORMALS)).start()
        enter[it, comp_me] = enter_out[it, n]

    def lines_step(it):
        zero = jnp.zeros((LINE, 128), F32)
        found = sweep(zero, zero, zero, zero)
        for c in range(COMP):
            for j, whole in enumerate(found):
                bounds[it, c, j] = whole[c * 8 : c * 8 + 8, :]
        for c in range(COMP):

            @pl.when(n != 3 * c)
            def _(c=c):
                b_copy(it, c).start()

        @pl.when(leader)
        def _():
            bounds_in[it, n] = bounds[it, comp_me]
            lead(it)

        if it == 0:
            finish_loads()
        for c in range(COMP):

            @pl.when(n != 3 * c)
            def _(c=c):
                e_arrival(it, c).wait_recv()

        entering = [
            jnp.concatenate([enter[it, c, j] for c in range(COMP)], axis=0) for j in range(4)
        ]
        sweep(*entering)

    def finish_loads():
        loads[12].wait()
        loads[13].wait()
        for half in range(2):
            for a in range(8):
                tile = iblank_v[half * 8 : half * 8 + 8, a * 128 : a * 128 + 128]
                active[pl.ds(half * 64 + a, 8, stride=8), :] = tile.astype(F32)

    def update(it):
        for i in range(ROWS):
            solved = [two_rows[i * LINE + m * 8 : i * LINE + m * 8 + 8, :] for m in range(COMP)]
            mask = active[i * 8 : i * 8 + 8, :]
            for c in range(COMP):
                total = right_v[c * COMP] * solved[0]
                for m in range(1, COMP):
                    total = total + right_v[c * COMP + m] * solved[m]
                at = slice(i * LINE + c * 8, i * LINE + c * 8 + 8)
                cur[at, :] = cur[at, :] + mask * total

    for it in range(ITERS):
        interpolate(it)
        if it == 0:
            prepare()
            prepare_mixing()
        place(it)
        start_y(it)
        finish_y(it)
        for i in range(2, ROWS - 2):
            source_row(it, i)

        @pl.when(n > 0)
        def _(it=it):
            z_copy(it, 0).wait_recv()

        @pl.when(n < NORMALS - 1)
        def _(it=it):
            z_copy(it, 1).wait_recv()

        for i in (0, 1, ROWS - 2, ROWS - 1):
            source_row(it, i)
        lines_step(it)

        @pl.when(n < NORMALS - 1)
        def _(it=it):
            z_copy(it, 0).wait_send()

        @pl.when(n > 0)
        def _(it=it):
            z_copy(it, 1).wait_send()

        update(it)

    for c in range(COMP):
        for half in range(2):
            for a in range(8):
                out[c, half * 8 : half * 8 + 8, a * 128 : a * 128 + 128] = cur[
                    pl.ds(half * 8 * LINE + c * 8 + a, 8, stride=LINE), :
                ]

    for it in range(ITERS):
        for k in ORDER:
            slot_copy(it, k).wait_send()

        @pl.when(s < SPANS - 1)
        def _(it=it):
            y_copy(it, 0).wait_send()

        @pl.when(s > 0)
        def _(it=it):
            y_copy(it, 1).wait_send()

        for c in range(COMP):

            @pl.when(n != 3 * c)
            def _(c=c, it=it):
                if it == 0:
                    mat_copy(c).wait_send()
                b_copy(it, c).wait_send()

        @pl.when(leader)
        def _(it=it):
            for off in range(1, NORMALS):
                e_copy(it, lax.rem(n + off, NORMALS)).wait_send()


def vmem(*shape, dtype=F32):
    return pltpu.VMEM(shape, dtype)


def local(
    state,
    iblank,
    flux,
    left_vectors,
    right_vectors,
    low_one,
    low_two,
    up_one,
    up_two,
    pivot,
    donor_cells,
    donor_weights,
    fringe_cells,
    fringe_live,
):
    dma = pltpu.SemaphoreType.DMA
    whole = ROWS * LINE
    slots = GRIDS * CAP
    out = pl.pallas_call(
        kernel,
        out_shape=jax.ShapeDtypeStruct((COMP, ROWS, 1024), F32),
        in_specs=[pl.BlockSpec(memory_space=pltpu.HBM)] * 14,
        out_specs=pl.BlockSpec(memory_space=pltpu.VMEM),
        scratch_shapes=[
            vmem(6, COMP, ROWS, 1024),
            vmem(ROWS, 1024, dtype=jnp.int32),
            vmem(COMP, 1, COMP),
            vmem(25, 8, 128),
            vmem(25, 8, 128),
            vmem(8 * slots, 128, dtype=jnp.int32),
            vmem(8 * slots, 128),
            vmem(slots, 128, dtype=jnp.int32),
            vmem(slots, 128, dtype=jnp.int32),
            vmem(whole, 128),
            vmem(whole, 128),
            vmem(whole, 128),
            vmem(whole, 128),
            vmem(whole, 128),
            vmem(whole, 128),
            vmem(ROWS * 8, 128),
            vmem(25, 8, 128),
            vmem(25, 8, 128),
            vmem(whole, 128),
            vmem(whole, 128),
            vmem(whole, 128),
            vmem(320, 512, dtype=BF16),
            vmem(256, 128),
            vmem(128, 128, dtype=jnp.int32),
            vmem(128, 128, dtype=jnp.int32),
            vmem(ITERS, 3, CAP * COMP, 128),
            vmem(ITERS, 3, CAP * COMP, 128),
            vmem(ITERS, 2, 8, 128),
            vmem(ITERS, 2, 8, 128),
            vmem(80, 128),
            vmem(80, 128),
            vmem(ITERS, 2 * LINE, 128),
            vmem(ITERS, 2 * LINE, 128),
            vmem(COMP, 12, 8, 128),
            vmem(NORMALS, 12, 8, 128),
            vmem(ITERS, COMP, 4, 8, 128),
            vmem(ITERS, NORMALS, 4, 8, 128),
            vmem(ITERS, NORMALS, 4, 8, 128),
            vmem(ITERS, COMP, 4, 8, 128),
            dma((14,)),
            dma((ITERS, 3)),
            dma((ITERS, 3)),
            dma((ITERS, 2)),
            dma((ITERS, 2)),
            dma((ITERS, 2)),
            dma((ITERS, 2)),
            dma((COMP,)),
            dma((NORMALS,)),
            dma((ITERS, COMP)),
            dma((ITERS, NORMALS)),
            dma((ITERS, NORMALS)),
            dma((ITERS, COMP)),
        ],
        compiler_params=pltpu.CompilerParams(
            collective_id=0, has_side_effects=True, vmem_limit_bytes=48 << 20
        ),
        name="adi_window",
    )(*(pltpu.with_memory_space_constraint(x, pltpu.HBM) for x in (
        state[:, 0],
        iblank[0],
        jnp.swapaxes(flux, 1, 2),
        left_vectors.reshape(25, 8, 128),
        right_vectors.reshape(25, 8, 128),
        low_one[:, 0],
        low_two[:, 0],
        up_one[:, 0],
        up_two[:, 0],
        pivot[:, 0],
        donor_cells.reshape(8 * slots, 128),
        donor_weights.reshape(8 * slots, 128),
        fringe_cells[0],
        fringe_live[0],
    )))
    return out[:, None]


def solution(mesh):
    cells = P(None, "grid", "normal", "span")
    slots = P("grid", "normal", "span")
    lines = P(None, None, "grid", "span")
    return jax.shard_map(
        local,
        mesh=mesh,
        in_specs=(
            cells,
            slots,
            P(None, None, "grid"),
            lines,
            lines,
            cells,
            cells,
            cells,
            cells,
            cells,
            cells,
            cells,
            slots,
            slots,
        ),
        out_specs=cells,
        check_vma=False,
    )
```

```python
import jax
import jax.numpy as jnp
from jax import lax
from jax.experimental import pallas as pl
from jax.experimental.pallas import tpu as pltpu
from jax.sharding import PartitionSpec as P

ITERS = 2
GRIDS = 4
SPANS = 4
NORMALS = 16
CAP = 6
SLOT_ROWS = GRIDS * CAP
ROWS = 16
COMP = 5
JOBS = 10
LINE = 40
ORDER = (2, 1, 3)
F32, BF16 = jnp.float32, jnp.bfloat16
LANE_GATHER = lax.GatherDimensionNumbers(
    offset_dims=(),
    collapsed_slice_dims=(1,),
    start_index_map=(1,),
    operand_batching_dims=(0,),
    start_indices_batching_dims=(0,),
)


def lane_gather(table, index):
    return lax.gather(
        table,
        index[:, :, None],
        LANE_GATHER,
        slice_sizes=(1, 1),
        mode=lax.GatherScatterMode.PROMISE_IN_BOUNDS,
    )


def leader_of(job):
    return lax.div(8 * job, 5) if not isinstance(job, int) else 8 * job // 5


def pack(x, y):
    upper = iota((8, 128), 0) < 4
    return jnp.where(upper, x, pltpu.roll(y, 4, 0)), jnp.where(upper, pltpu.roll(x, 4, 0), y)


def iota(shape, dim):
    return lax.broadcasted_iota(jnp.int32, shape, dim)


def to_lines(raw, lines):
    for c in range(COMP):
        for half in range(2):
            for a in range(8):
                tile = raw[c, half * 8 : half * 8 + 8, a * 128 : a * 128 + 128]
                lines[pl.ds(half * 8 * LINE + c * 8 + a, 8, stride=LINE), :] = tile


def kernel(
    state,
    iblank,
    flux,
    left,
    right,
    low_one,
    low_two,
    up_one,
    up_two,
    pivot,
    donor_cells,
    donor_weights,
    fringe_cells,
    fringe_live,
    out,
    raw,
    iblank_v,
    flux_v,
    left_v,
    right_v,
    cells_v,
    weights_v,
    fringe_v,
    live_v,
    cur,
    low1,
    low2,
    up1,
    up2,
    piv,
    active,
    mix_c,
    mix_d,
    src,
    one_rows,
    two_rows,
    table,
    inverse,
    inv_row,
    inv_lane,
    sent,
    received,
    ysend,
    yrecv,
    halo_l,
    halo_r,
    zlo,
    zhi,
    mats,
    mats_in,
    bounds,
    bounds_in,
    enter_out,
    enter,
    in_sem,
    slot_ssem,
    slot_rsem,
    y_ssem,
    y_rsem,
    z_ssem,
    z_rsem,
    mat_ssem,
    mat_rsem,
    b_ssem,
    b_rsem,
    e_ssem,
    e_rsem,
):
    g = lax.axis_index("grid")
    s = lax.axis_index("span")
    n = lax.axis_index("normal")
    job = lax.div(5 * n + 7, 8)
    leader = jnp.logical_and(job < JOBS, leader_of(job) == n)
    visits = [lax.rem(lax.div(5 * n, 8) + off, JOBS) for off in (5, 4, 6, 3, 7, 2, 8, 1, 9, 0)]

    pairs = [
        (state, raw.at[0]),
        (donor_cells, cells_v),
        (donor_weights, weights_v),
        (low_one, raw.at[1]),
        (low_two, raw.at[2]),
        (up_one, raw.at[3]),
        (up_two, raw.at[4]),
        (pivot, raw.at[5]),
        (fringe_cells, fringe_v),
        (fringe_live, live_v),
        (left, left_v),
        (flux, flux_v),
        (right, right_v),
        (iblank, iblank_v),
    ]
    loads = [pltpu.make_async_copy(a, b, in_sem.at[k]) for k, (a, b) in enumerate(pairs)]
    for load in loads:
        load.start()

    barrier = pltpu.get_barrier_semaphore()
    for k in range(1, GRIDS):
        pl.semaphore_signal(barrier, inc=1, device_id={"grid": lax.rem(g + k, GRIDS)})
    for k in range(1, NORMALS):
        pl.semaphore_signal(barrier, inc=1, device_id={"normal": lax.rem(n + k, NORMALS)})

    for k in (1, SPANS - 1):
        pl.semaphore_signal(barrier, inc=1, device_id={"span": lax.rem(s + k, SPANS)})

    def barrier_wait():
        pl.semaphore_wait(barrier, GRIDS - 1 + NORMALS - 1 + 2)

    zeros8 = jnp.zeros((8, 128), F32)

    @pl.when(s == 0)
    def _():
        for it in range(ITERS):
            yrecv[it, 0] = zeros8

    @pl.when(s == SPANS - 1)
    def _():
        for it in range(ITERS):
            yrecv[it, 1] = zeros8

    @pl.when(n == 0)
    def _():
        for it in range(ITERS):
            zlo[it] = jnp.zeros((2 * LINE, 128), F32)

    @pl.when(n == NORMALS - 1)
    def _():
        for it in range(ITERS):
            zhi[it] = jnp.zeros((2 * LINE, 128), F32)

    loads[0].wait()
    to_lines(raw.at[0], cur)
    loads[1].wait()
    loads[2].wait()

    def slot_copy(it, k):
        return pltpu.make_async_remote_copy(
            src_ref=sent.at[it, k - 1],
            dst_ref=received.at[it, k - 1],
            send_sem=slot_ssem.at[it, k - 1],
            recv_sem=slot_rsem.at[it, k - 1],
            device_id={"grid": lax.rem(g + k, GRIDS)},
            device_id_type=pl.DeviceIdType.MESH,
        )

    def y_copy(it, side):
        return pltpu.make_async_remote_copy(
            src_ref=ysend.at[it, side],
            dst_ref=yrecv.at[it, side],
            send_sem=y_ssem.at[it, side],
            recv_sem=y_rsem.at[it, side],
            device_id={"span": s + (1 if side == 0 else -1)},
            device_id_type=pl.DeviceIdType.MESH,
        )

    def z_copy(it, side):
        return pltpu.make_async_remote_copy(
            src_ref=cur.at[pl.ds((ROWS - 2) * LINE if side == 0 else 0, 2 * LINE), :],
            dst_ref=(zlo if side == 0 else zhi).at[it],
            send_sem=z_ssem.at[it, side],
            recv_sem=z_rsem.at[it, side],
            device_id={"normal": n + (1 if side == 0 else -1)},
            device_id_type=pl.DeviceIdType.MESH,
        )

    def to_leader(source, target, ssem, rsem, peer):
        return pltpu.make_async_remote_copy(
            src_ref=source,
            dst_ref=target,
            send_sem=ssem,
            recv_sem=rsem,
            device_id={"normal": peer},
            device_id_type=pl.DeviceIdType.MESH,
        )

    def mat_copy(j):
        return to_leader(mats.at[j], mats_in.at[n], mat_ssem.at[j], mat_rsem.at[n], leader_of(j))

    def mat_arrival(k):
        return to_leader(mats.at[0], mats_in.at[k], mat_ssem.at[0], mat_rsem.at[k], k)

    def b_copy(it, j):
        return to_leader(
            bounds.at[it, j], bounds_in.at[it, n], b_ssem.at[it, j], b_rsem.at[it, n], leader_of(j)
        )

    def b_arrival(it, k):
        return to_leader(
            bounds.at[it, 0], bounds_in.at[it, k], b_ssem.at[it, 0], b_rsem.at[it, k], k
        )

    def e_copy(it, k):
        return to_leader(
            enter_out.at[it, k], enter.at[it, job], e_ssem.at[it, k], e_rsem.at[it, job], k
        )

    def e_arrival(it, j):
        return to_leader(
            enter_out.at[it, 0], enter.at[it, j], e_ssem.at[it, 0], e_rsem.at[it, j], leader_of(j)
        )

    def one_hot_pair(row, pair, total):
        cells = [cells_v[pl.ds((2 * pair + e) * SLOT_ROWS + row, 1), :] for e in range(2)]
        parts = []
        for cell in cells:
            low = ((cell >> 10) & 1) * 128 + (cell & 127)
            low = jnp.broadcast_to(low.astype(F32).astype(BF16), (256, 128))
            rank = iota((256, 128), 0).astype(F32).astype(BF16)
            parts.append(jnp.where(rank == low, jnp.ones((), BF16), jnp.zeros((), BF16)))
        hot = jnp.concatenate(parts, axis=1)
        found = jnp.dot(
            table[...], jnp.concatenate([hot, hot], axis=0), preferred_element_type=F32
        )
        for e in range(2):
            high = ((cells[e] >> 11) << 3) | ((cells[e] >> 7) & 7)
            weight = jnp.broadcast_to(
                weights_v[pl.ds((2 * pair + e) * SLOT_ROWS + row, 1), :], (8, 128)
            )
            for v in range(8):
                mask = jnp.where(iota((8, 128), 0) + v * 8 == high, weight, 0.0)
                for c in range(COMP):
                    at = c * 64 + v * 8
                    total[c] = total[c] + found[at : at + 8, e * 128 : e * 128 + 128] * mask

    def interpolate(it):
        for c in range(COMP):
            for m in range(0, 8, 2):
                for p in range(2):
                    x = jnp.concatenate(
                        [
                            cur[(2 * m + p) * LINE + c * 8 : (2 * m + p) * LINE + c * 8 + 8, :],
                            cur[(2 * m + 2 + p) * LINE + c * 8 : (2 * m + 2 + p) * LINE + c * 8 + 8, :],
                        ],
                        axis=0,
                    )
                    head = x.astype(BF16)
                    tail = (x - head.astype(F32)).astype(BF16)
                    rows = slice(c * 64 + m * 8, c * 64 + m * 8 + 16)
                    table[rows, p * 128 : p * 128 + 128] = head
                    table[rows, 256 + p * 128 : 256 + p * 128 + 128] = tail
        for turn, k in enumerate(ORDER):
            receiver = lax.rem(g + k, GRIDS)

            def three_rows(trip, _, k=k, receiver=receiver):
                first = receiver * CAP + 3 * trip
                cells = cells_v[pl.ds(first + 2, 8, stride=SLOT_ROWS), :]
                lanes, blocks = cells & 127, cells >> 7
                picked = [zeros8] * COMP
                sums = [[zeros8] * COMP for _ in range(2)]
                for step in range(8):
                    one_hot_pair(first + step // 4, step % 4, sums[step // 4])
                    for block in range(16 * step, 16 * step + 16):
                        hit = blocks == block
                        at = (block // 8) * LINE + block % 8
                        for c in range(COMP):
                            values = cur[pl.ds(at + c * 8, 8, stride=0), :]
                            picked[c] = jnp.where(hit, lane_gather(values, lanes), picked[c])
                weight = weights_v[pl.ds(first + 2, 8, stride=SLOT_ROWS), :]
                sums.append([p * weight for p in picked])
                for e in range(3):
                    for c in range(COMP):
                        sent[it, k - 1, pl.ds((3 * trip + e) * COMP + c, 1), :] = jnp.sum(
                            sums[e][c], axis=0, keepdims=True
                        )
                return 0

            lax.fori_loop(0, CAP // 3, three_rows, 0)
            if it == 0 and turn == 0:
                load_coefficients()
                barrier_wait()
            slot_copy(it, k).start()
            if it == 0 and turn == 0:
                send_matrices()

    def invert_fringe():
        total = jnp.zeros((256, 128), F32)
        lane = iota((128, 128), 1).astype(F32)
        place_of = iota((128, 128), 0)
        for k in ORDER:
            source = lax.rem(g + GRIDS - k, GRIDS)
            named, columns = [], []
            for b in range(CAP):
                row = source * CAP + b
                cell = fringe_v[pl.ds(row, 1), :]
                live = live_v[pl.ds(row, 1), :]
                high = jnp.where(live == 1, cell >> 7, -1)
                low = cell & 127
                hit = place_of == high
                number = float((k - 1) * CAP + b + 1)
                named.append(
                    jnp.concatenate(
                        [jnp.where(hit, number, 0.0), jnp.where(hit, lane, 0.0)], axis=0
                    ).astype(BF16)
                )
                columns.append(jnp.where(place_of == low, 1.0, 0.0).astype(BF16))
            total = total + lax.dot_general(
                jnp.concatenate(named, axis=1),
                jnp.concatenate(columns, axis=1),
                (((1,), (1,)), ((), ())),
                preferred_element_type=F32,
            )
        inverse[...] = total
        inv_row[...] = inverse[0:128, :].astype(jnp.int32) - 1
        inv_lane[...] = inverse[128:256, :].astype(jnp.int32)

    def line(ref, i):
        return ref[i * LINE : i * LINE + LINE, :]

    def block_matrices():
        zero = jnp.zeros((LINE, 128), F32)
        ones = jnp.ones((LINE, 128), F32)
        a1, a2, b1, b2 = ones, zero, zero, ones
        for i in range(ROWS):
            c1, c2 = line(low1, i), line(low2, i)
            a1, a2 = -c1 * a1 - c2 * a2, a1
            b1, b2 = -c1 * b1 - c2 * b2, b1
            one_rows[i * LINE : i * LINE + LINE, :] = a1
            two_rows[i * LINE : i * LINE + LINE, :] = b1
        found = [a1, b1, a2, b2]
        a1, a2, b1, b2 = ones, zero, zero, ones
        p1 = p2 = q1 = q2 = zero
        for i in reversed(range(ROWS)):
            c1, c2, pv = line(up1, i), line(up2, i), line(piv, i)
            a1, a2 = -c1 * a1 - c2 * a2, a1
            b1, b2 = -c1 * b1 - c2 * b2, b1
            p1, p2 = pv * line(one_rows, i) - c1 * p1 - c2 * p2, p1
            q1, q2 = pv * line(two_rows, i) - c1 * q1 - c2 * q2, q1
        found += [a1, b1, a2, b2, p1, q1, p2, q2]
        for c in range(COMP):
            part = [whole[c * 8 : c * 8 + 8, :] for whole in found]
            for j in range(0, 12, 4):
                for half, packed in enumerate(pack(part[j], part[j + 3])):
                    mats[2 * c + half, j // 2] = packed
                for half, packed in enumerate(pack(part[j + 1], part[j + 2])):
                    mats[2 * c + half, j // 2 + 1] = packed

    def load_coefficients():
        for k, lines in ((3, low1), (4, low2), (5, up1), (6, up2), (7, piv)):
            loads[k].wait()
            to_lines(raw.at[k - 2], lines)
        block_matrices()

    def send_matrices():
        for j in visits:

            @pl.when(leader_of(j) != n)
            def _(j=j):
                mat_copy(j).start()

        @pl.when(leader)
        def _():
            mats_in[n] = mats[job]

    def prepare():
        loads[8].wait()
        loads[9].wait()
        invert_fringe()

    def prepare_mixing():
        loads[10].wait()
        loads[11].wait()
        f = [[jnp.broadcast_to(flux_v[k, :, m : m + 1], (8, 128)) for m in range(COMP)] for k in range(COMP)]
        for c in range(COMP):
            row = [left_v[c * COMP + k] for k in range(COMP)]
            for m in range(COMP):
                total = row[0] * f[0][m]
                for k in range(1, COMP):
                    total = total + row[k] * f[k][m]
                mix_c[c * COMP + m] = total * -0.2
                mix_d[c * COMP + m] = row[m] * -0.024

    def place_rows(it, k, i_list):
        for i in i_list:
            lanes = inv_lane[i * 8 : i * 8 + 8, :]
            rows = inv_row[i * 8 : i * 8 + 8, :]
            values = [cur[i * LINE + c * 8 : i * LINE + c * 8 + 8, :] for c in range(COMP)]
            for b in range(CAP):
                hit = rows == (k - 1) * CAP + b
                for c in range(COMP):
                    slots = received[it, k - 1, pl.ds(b * COMP + c, 8, stride=0), :]
                    values[c] = jnp.where(hit, lane_gather(slots, lanes), values[c])
            for c in range(COMP):
                cur[i * LINE + c * 8 : i * LINE + c * 8 + 8, :] = values[c]

    def place(it):
        for turn, k in enumerate(ORDER):
            slot_copy(it, k).wait_recv()
            if turn == GRIDS - 2:
                place_rows(it, k, (0, 1, 14, 15))
                start_z(it)
                place_rows(it, k, range(2, 14))
            else:
                place_rows(it, k, range(ROWS))

    def start_z(it):
        @pl.when(n < NORMALS - 1)
        def _():
            z_copy(it, 0).start()

        @pl.when(n > 0)
        def _():
            z_copy(it, 1).start()

    def start_y(it):
        lane = iota((8, 128), 1)
        for side in range(2):
            total = zeros8
            for m in range(10):
                rows = cur[pl.ds(m * 64 + (7 if side == 0 else 0), 8, stride=8), :]
                shift = (2 * m + (2 if side == 0 else 0)) % 128
                rows = pltpu.roll(rows, shift, 1) if shift else rows
                total = jnp.where((lane >> 1) == m, rows, total)
            ysend[it, side] = total

        @pl.when(s < SPANS - 1)
        def _():
            y_copy(it, 0).start()

        @pl.when(s > 0)
        def _():
            y_copy(it, 1).start()

    def finish_y(it):
        @pl.when(s > 0)
        def _():
            y_copy(it, 0).wait_recv()

        @pl.when(s < SPANS - 1)
        def _():
            y_copy(it, 1).wait_recv()

        for side, halo in ((0, halo_l), (1, halo_r)):
            packed = yrecv[it, side]
            for m in range(10):
                shift = (126 - 2 * m) if side == 0 else (128 - 2 * m) % 128
                halo[m * 8 : m * 8 + 8, :] = pltpu.roll(packed, shift, 1) if shift else packed

    def source_row(it, i):
        lane = iota((8, 128), 1)
        sub = iota((8, 128), 0)

        def at(row, c):
            if row < 0:
                return zlo[it, (row + 2) * LINE + c * 8 : (row + 2) * LINE + c * 8 + 8, :]
            if row >= ROWS:
                return zhi[it, (row - ROWS) * LINE + c * 8 : (row - ROWS) * LINE + c * 8 + 8, :]
            return cur[row * LINE + c * 8 : row * LINE + c * 8 + 8, :]

        central, fourth = [], []
        for c in range(COMP):
            x = at(i, c)
            above = jnp.where(
                sub == 7, halo_r[pl.ds(i * COMP + c, 8, stride=0), :], pltpu.roll(x, 7, 0)
            )
            below = jnp.where(
                sub == 0, halo_l[pl.ds(i * COMP + c, 8, stride=0), :], pltpu.roll(x, 1, 0)
            )
            plus1 = pltpu.roll(jnp.where(lane < 1, above, x), 127, 1)
            plus2 = pltpu.roll(jnp.where(lane < 2, above, x), 126, 1)
            minus1 = pltpu.roll(jnp.where(lane >= 127, below, x), 1, 1)
            minus2 = pltpu.roll(jnp.where(lane >= 126, below, x), 2, 1)
            central.append(plus1 - minus1)
            near = (plus1 + minus1) + (at(i + 1, c) + at(i - 1, c))
            far = (plus2 + minus2) + (at(i + 2, c) + at(i - 2, c))
            fourth.append(far - 4.0 * near + 12.0 * x)
        for c in range(COMP):
            total = mix_c[c * COMP] * central[0] + mix_d[c * COMP] * fourth[0]
            for m in range(1, COMP):
                total = total + mix_c[c * COMP + m] * central[m] + mix_d[c * COMP + m] * fourth[m]
            src[i * LINE + c * 8 : i * LINE + c * 8 + 8, :] = total

    def sweep(e1, e2, f1, f2):
        for i in range(ROWS):
            e1, e2 = line(src, i) - line(low1, i) * e1 - line(low2, i) * e2, e1
            one_rows[i * LINE : i * LINE + LINE, :] = e1
        for i in reversed(range(ROWS)):
            f1, f2 = line(piv, i) * line(one_rows, i) - line(up1, i) * f1 - line(up2, i) * f2, f1
            two_rows[i * LINE : i * LINE + LINE, :] = f1
        return e1, e2, f1, f2

    def lead(it):
        def arrive(k, _):
            @pl.when(k != n)
            def _():
                if it == 0:
                    mat_arrival(k).wait_recv()
                b_arrival(it, k).wait_recv()

            return 0

        lax.fori_loop(0, NORMALS, arrive, 0)
        def apply(k, at, x):
            return mats_in[k, at] * x + mats_in[k, at + 1] * pltpu.roll(x, 4, 0)

        x = zeros8
        pushed = []
        for k in range(NORMALS):
            enter_out[it, k, 0] = x
            pushed.append(apply(k, 4, x) + bounds_in[it, k, 1])
            x = apply(k, 0, x) + bounds_in[it, k, 0]
        x = zeros8
        for k in reversed(range(NORMALS)):
            enter_out[it, k, 1] = x
            x = apply(k, 2, x) + pushed[k]
        for far in range(8, 0, -1):
            for off in {far, NORMALS - far}:
                e_copy(it, lax.rem(n + off, NORMALS)).start()
        enter[it, job] = enter_out[it, n]

    def lines_step(it):
        zero = jnp.zeros((LINE, 128), F32)
        found = sweep(zero, zero, zero, zero)
        for c in range(COMP):
            part = [whole[c * 8 : c * 8 + 8, :] for whole in found]
            for way in range(2):
                for half, packed in enumerate(pack(part[2 * way], part[2 * way + 1])):
                    bounds[it, 2 * c + half, way] = packed
        for j in visits:

            @pl.when(leader_of(j) != n)
            def _(j=j):
                b_copy(it, j).start()

        @pl.when(leader)
        def _():
            bounds_in[it, n] = bounds[it, job]
            lead(it)

        if it == 0:
            finish_loads()
        for j in range(JOBS):

            @pl.when(n != leader_of(j))
            def _(j=j):
                e_arrival(it, j).wait_recv()

        entering = [[], [], [], []]
        for c in range(COMP):
            for way in range(2):
                x, y = pack(enter[it, 2 * c, way], enter[it, 2 * c + 1, way])
                entering[2 * way].append(x)
                entering[2 * way + 1].append(y)
        entering = [jnp.concatenate(parts, axis=0) for parts in entering]
        sweep(*entering)

    def finish_loads():
        loads[12].wait()
        loads[13].wait()
        for half in range(2):
            for a in range(8):
                tile = iblank_v[half * 8 : half * 8 + 8, a * 128 : a * 128 + 128]
                active[pl.ds(half * 64 + a, 8, stride=8), :] = tile.astype(F32)

    def update(it):
        for i in range(ROWS):
            solved = [two_rows[i * LINE + m * 8 : i * LINE + m * 8 + 8, :] for m in range(COMP)]
            mask = active[i * 8 : i * 8 + 8, :]
            for c in range(COMP):
                total = right_v[c * COMP] * solved[0]
                for m in range(1, COMP):
                    total = total + right_v[c * COMP + m] * solved[m]
                at = slice(i * LINE + c * 8, i * LINE + c * 8 + 8)
                cur[at, :] = cur[at, :] + mask * total

    for it in range(ITERS):
        interpolate(it)
        if it == 0:
            prepare()
            prepare_mixing()
        place(it)
        start_y(it)
        finish_y(it)
        for i in range(2, ROWS - 2):
            source_row(it, i)

        @pl.when(n > 0)
        def _(it=it):
            z_copy(it, 0).wait_recv()

        @pl.when(n < NORMALS - 1)
        def _(it=it):
            z_copy(it, 1).wait_recv()

        for i in (0, 1, ROWS - 2, ROWS - 1):
            source_row(it, i)
        lines_step(it)

        @pl.when(n < NORMALS - 1)
        def _(it=it):
            z_copy(it, 0).wait_send()

        @pl.when(n > 0)
        def _(it=it):
            z_copy(it, 1).wait_send()

        update(it)

    for c in range(COMP):
        for half in range(2):
            for a in range(8):
                out[c, half * 8 : half * 8 + 8, a * 128 : a * 128 + 128] = cur[
                    pl.ds(half * 8 * LINE + c * 8 + a, 8, stride=LINE), :
                ]

    for it in range(ITERS):
        for k in ORDER:
            slot_copy(it, k).wait_send()

        @pl.when(s < SPANS - 1)
        def _(it=it):
            y_copy(it, 0).wait_send()

        @pl.when(s > 0)
        def _(it=it):
            y_copy(it, 1).wait_send()

        for j in range(JOBS):

            @pl.when(n != leader_of(j))
            def _(j=j, it=it):
                if it == 0:
                    mat_copy(j).wait_send()
                b_copy(it, j).wait_send()

        @pl.when(leader)
        def _(it=it):
            for off in range(1, NORMALS):
                e_copy(it, lax.rem(n + off, NORMALS)).wait_send()


def vmem(*shape, dtype=F32):
    return pltpu.VMEM(shape, dtype)


def local(
    state,
    iblank,
    flux,
    left_vectors,
    right_vectors,
    low_one,
    low_two,
    up_one,
    up_two,
    pivot,
    donor_cells,
    donor_weights,
    fringe_cells,
    fringe_live,
):
    dma = pltpu.SemaphoreType.DMA
    whole = ROWS * LINE
    slots = GRIDS * CAP
    out = pl.pallas_call(
        kernel,
        out_shape=jax.ShapeDtypeStruct((COMP, ROWS, 1024), F32),
        in_specs=[pl.BlockSpec(memory_space=pltpu.HBM)] * 14,
        out_specs=pl.BlockSpec(memory_space=pltpu.VMEM),
        scratch_shapes=[
            vmem(6, COMP, ROWS, 1024),
            vmem(ROWS, 1024, dtype=jnp.int32),
            vmem(COMP, 1, COMP),
            vmem(25, 8, 128),
            vmem(25, 8, 128),
            vmem(8 * slots, 128, dtype=jnp.int32),
            vmem(8 * slots, 128),
            vmem(slots, 128, dtype=jnp.int32),
            vmem(slots, 128, dtype=jnp.int32),
            vmem(whole, 128),
            vmem(whole, 128),
            vmem(whole, 128),
            vmem(whole, 128),
            vmem(whole, 128),
            vmem(whole, 128),
            vmem(ROWS * 8, 128),
            vmem(25, 8, 128),
            vmem(25, 8, 128),
            vmem(whole, 128),
            vmem(whole, 128),
            vmem(whole, 128),
            vmem(320, 512, dtype=BF16),
            vmem(256, 128),
            vmem(128, 128, dtype=jnp.int32),
            vmem(128, 128, dtype=jnp.int32),
            vmem(ITERS, 3, CAP * COMP, 128),
            vmem(ITERS, 3, CAP * COMP, 128),
            vmem(ITERS, 2, 8, 128),
            vmem(ITERS, 2, 8, 128),
            vmem(80, 128),
            vmem(80, 128),
            vmem(ITERS, 2 * LINE, 128),
            vmem(ITERS, 2 * LINE, 128),
            vmem(JOBS, 6, 8, 128),
            vmem(NORMALS, 6, 8, 128),
            vmem(ITERS, JOBS, 2, 8, 128),
            vmem(ITERS, NORMALS, 2, 8, 128),
            vmem(ITERS, NORMALS, 2, 8, 128),
            vmem(ITERS, JOBS, 2, 8, 128),
            dma((14,)),
            dma((ITERS, 3)),
            dma((ITERS, 3)),
            dma((ITERS, 2)),
            dma((ITERS, 2)),
            dma((ITERS, 2)),
            dma((ITERS, 2)),
            dma((JOBS,)),
            dma((NORMALS,)),
            dma((ITERS, JOBS)),
            dma((ITERS, NORMALS)),
            dma((ITERS, NORMALS)),
            dma((ITERS, JOBS)),
        ],
        compiler_params=pltpu.CompilerParams(
            collective_id=0, has_side_effects=True, vmem_limit_bytes=48 << 20
        ),
        name="adi_window",
    )(*(pltpu.with_memory_space_constraint(x, pltpu.HBM) for x in (
        state[:, 0],
        iblank[0],
        jnp.swapaxes(flux, 1, 2),
        left_vectors.reshape(25, 8, 128),
        right_vectors.reshape(25, 8, 128),
        low_one[:, 0],
        low_two[:, 0],
        up_one[:, 0],
        up_two[:, 0],
        pivot[:, 0],
        donor_cells.reshape(8 * slots, 128),
        donor_weights.reshape(8 * slots, 128),
        fringe_cells[0],
        fringe_live[0],
    )))
    return out[:, None]


def solution(mesh):
    cells = P(None, "grid", "normal", "span")
    slots = P("grid", "normal", "span")
    lines = P(None, None, "grid", "span")
    return jax.shard_map(
        local,
        mesh=mesh,
        in_specs=(
            cells,
            slots,
            P(None, None, "grid"),
            lines,
            lines,
            cells,
            cells,
            cells,
            cells,
            cells,
            cells,
            cells,
            slots,
            slots,
        ),
        out_specs=cells,
        check_vma=False,
    )
```

```python
import jax
import jax.numpy as jnp
from jax import lax
from jax.experimental import pallas as pl
from jax.experimental.pallas import tpu as pltpu
from jax.sharding import PartitionSpec as P

ITERS = 2
GRIDS = 4
SPANS = 4
NORMALS = 16
CAP = 6
SLOT_ROWS = GRIDS * CAP
ROWS = 16
COMP = 5
JOBS = 10
LINE = 40
ORDER = (2, 1, 3)
F32, BF16 = jnp.float32, jnp.bfloat16
LANE_GATHER = lax.GatherDimensionNumbers(
    offset_dims=(),
    collapsed_slice_dims=(1,),
    start_index_map=(1,),
    operand_batching_dims=(0,),
    start_indices_batching_dims=(0,),
)


def lane_gather(table, index):
    return lax.gather(
        table,
        index[:, :, None],
        LANE_GATHER,
        slice_sizes=(1, 1),
        mode=lax.GatherScatterMode.PROMISE_IN_BOUNDS,
    )


def leader_of(job):
    return lax.div(8 * job, 5) if not isinstance(job, int) else 8 * job // 5


def pack(x, y):
    upper = iota((8, 128), 0) < 4
    return jnp.where(upper, x, pltpu.roll(y, 4, 0)), jnp.where(upper, pltpu.roll(x, 4, 0), y)


def iota(shape, dim):
    return lax.broadcasted_iota(jnp.int32, shape, dim)


def to_lines(raw, lines):
    for c in range(COMP):
        for half in range(2):
            for a in range(8):
                tile = raw[c, half * 8 : half * 8 + 8, a * 128 : a * 128 + 128]
                lines[pl.ds(half * 8 * LINE + c * 8 + a, 8, stride=LINE), :] = tile


def kernel(
    state,
    iblank,
    flux,
    left,
    right,
    low_one,
    low_two,
    up_one,
    up_two,
    pivot,
    donor_cells,
    donor_weights,
    fringe_cells,
    fringe_live,
    out,
    raw,
    iblank_v,
    flux_v,
    left_v,
    right_v,
    cells_v,
    weights_v,
    fringe_v,
    live_v,
    cur,
    low1,
    low2,
    up1,
    up2,
    piv,
    active,
    mix_c,
    mix_d,
    src,
    one_rows,
    two_rows,
    table,
    inverse,
    inv_row,
    inv_lane,
    sent,
    received,
    ysend,
    yrecv,
    halo_l,
    halo_r,
    zlo,
    zhi,
    mats,
    mats_in,
    bounds,
    bounds_in,
    enter_out,
    enter,
    in_sem,
    slot_ssem,
    slot_rsem,
    y_ssem,
    y_rsem,
    z_ssem,
    z_rsem,
    mat_ssem,
    mat_rsem,
    b_ssem,
    b_rsem,
    e_ssem,
    e_rsem,
):
    g = lax.axis_index("grid")
    s = lax.axis_index("span")
    n = lax.axis_index("normal")
    job = lax.div(5 * n + 7, 8)
    leader = jnp.logical_and(job < JOBS, leader_of(job) == n)
    visits = [lax.rem(lax.div(5 * n, 8) + off, JOBS) for off in (5, 4, 6, 3, 7, 2, 8, 1, 9, 0)]

    pairs = [
        (state, raw.at[0]),
        (donor_cells, cells_v),
        (donor_weights, weights_v),
        (low_one, raw.at[1]),
        (low_two, raw.at[2]),
        (up_one, raw.at[3]),
        (up_two, raw.at[4]),
        (pivot, raw.at[5]),
        (fringe_cells, fringe_v),
        (fringe_live, live_v),
        (left, left_v),
        (flux, flux_v),
        (right, right_v),
        (iblank, iblank_v),
    ]
    loads = [pltpu.make_async_copy(a, b, in_sem.at[k]) for k, (a, b) in enumerate(pairs)]
    for load in loads:
        load.start()

    barrier = pltpu.get_barrier_semaphore()
    for k in range(1, GRIDS):
        pl.semaphore_signal(barrier, inc=1, device_id={"grid": lax.rem(g + k, GRIDS)})
    for k in range(1, NORMALS):
        pl.semaphore_signal(barrier, inc=1, device_id={"normal": lax.rem(n + k, NORMALS)})

    for k in (1, SPANS - 1):
        pl.semaphore_signal(barrier, inc=1, device_id={"span": lax.rem(s + k, SPANS)})

    def barrier_wait():
        pl.semaphore_wait(barrier, GRIDS - 1 + NORMALS - 1 + 2)

    zeros8 = jnp.zeros((8, 128), F32)

    @pl.when(s == 0)
    def _():
        for it in range(ITERS):
            yrecv[it, 0] = zeros8

    @pl.when(s == SPANS - 1)
    def _():
        for it in range(ITERS):
            yrecv[it, 1] = zeros8

    @pl.when(n == 0)
    def _():
        for it in range(ITERS):
            zlo[it] = jnp.zeros((2 * LINE, 128), F32)

    @pl.when(n == NORMALS - 1)
    def _():
        for it in range(ITERS):
            zhi[it] = jnp.zeros((2 * LINE, 128), F32)

    loads[0].wait()
    to_lines(raw.at[0], cur)
    loads[1].wait()
    loads[2].wait()

    def slot_copy(it, k, half):
        return pltpu.make_async_remote_copy(
            src_ref=sent.at[it, k - 1, half],
            dst_ref=received.at[it, k - 1, half],
            send_sem=slot_ssem.at[it, k - 1, half],
            recv_sem=slot_rsem.at[it, k - 1, half],
            device_id={"grid": lax.rem(g + k, GRIDS)},
            device_id_type=pl.DeviceIdType.MESH,
        )

    def y_copy(it, side):
        return pltpu.make_async_remote_copy(
            src_ref=ysend.at[it, side],
            dst_ref=yrecv.at[it, side],
            send_sem=y_ssem.at[it, side],
            recv_sem=y_rsem.at[it, side],
            device_id={"span": s + (1 if side == 0 else -1)},
            device_id_type=pl.DeviceIdType.MESH,
        )

    def z_copy(it, side):
        return pltpu.make_async_remote_copy(
            src_ref=cur.at[pl.ds((ROWS - 2) * LINE if side == 0 else 0, 2 * LINE), :],
            dst_ref=(zlo if side == 0 else zhi).at[it],
            send_sem=z_ssem.at[it, side],
            recv_sem=z_rsem.at[it, side],
            device_id={"normal": n + (1 if side == 0 else -1)},
            device_id_type=pl.DeviceIdType.MESH,
        )

    def to_leader(source, target, ssem, rsem, peer):
        return pltpu.make_async_remote_copy(
            src_ref=source,
            dst_ref=target,
            send_sem=ssem,
            recv_sem=rsem,
            device_id={"normal": peer},
            device_id_type=pl.DeviceIdType.MESH,
        )

    def mat_copy(j):
        return to_leader(mats.at[j], mats_in.at[n], mat_ssem.at[j], mat_rsem.at[n], leader_of(j))

    def mat_arrival(k):
        return to_leader(mats.at[0], mats_in.at[k], mat_ssem.at[0], mat_rsem.at[k], k)

    def b_copy(it, j):
        return to_leader(
            bounds.at[it, j], bounds_in.at[it, n], b_ssem.at[it, j], b_rsem.at[it, n], leader_of(j)
        )

    def b_arrival(it, k):
        return to_leader(
            bounds.at[it, 0], bounds_in.at[it, k], b_ssem.at[it, 0], b_rsem.at[it, k], k
        )

    def e_copy(it, k):
        return to_leader(
            enter_out.at[it, k], enter.at[it, job], e_ssem.at[it, k], e_rsem.at[it, job], k
        )

    def e_arrival(it, j):
        return to_leader(
            enter_out.at[it, 0], enter.at[it, j], e_ssem.at[it, 0], e_rsem.at[it, j], leader_of(j)
        )

    def one_hot_pair(row, pair, total):
        cells = [cells_v[pl.ds((2 * pair + e) * SLOT_ROWS + row, 1), :] for e in range(2)]
        parts = []
        for cell in cells:
            low = ((cell >> 10) & 1) * 128 + (cell & 127)
            low = jnp.broadcast_to(low.astype(F32).astype(BF16), (256, 128))
            rank = iota((256, 128), 0).astype(F32).astype(BF16)
            parts.append(jnp.where(rank == low, jnp.ones((), BF16), jnp.zeros((), BF16)))
        hot = jnp.concatenate(parts, axis=1)
        found = jnp.dot(
            table[...], jnp.concatenate([hot, hot], axis=0), preferred_element_type=F32
        )
        for e in range(2):
            high = ((cells[e] >> 11) << 3) | ((cells[e] >> 7) & 7)
            weight = jnp.broadcast_to(
                weights_v[pl.ds((2 * pair + e) * SLOT_ROWS + row, 1), :], (8, 128)
            )
            for v in range(8):
                mask = jnp.where(iota((8, 128), 0) + v * 8 == high, weight, 0.0)
                for c in range(COMP):
                    at = c * 64 + v * 8
                    total[c] = total[c] + found[at : at + 8, e * 128 : e * 128 + 128] * mask

    def interpolate(it):
        for c in range(COMP):
            for m in range(0, 8, 2):
                for p in range(2):
                    x = jnp.concatenate(
                        [
                            cur[(2 * m + p) * LINE + c * 8 : (2 * m + p) * LINE + c * 8 + 8, :],
                            cur[(2 * m + 2 + p) * LINE + c * 8 : (2 * m + 2 + p) * LINE + c * 8 + 8, :],
                        ],
                        axis=0,
                    )
                    head = x.astype(BF16)
                    tail = (x - head.astype(F32)).astype(BF16)
                    rows = slice(c * 64 + m * 8, c * 64 + m * 8 + 16)
                    table[rows, p * 128 : p * 128 + 128] = head
                    table[rows, 256 + p * 128 : 256 + p * 128 + 128] = tail
        for turn, k in enumerate(ORDER):
            receiver = lax.rem(g + k, GRIDS)

            def three_rows(trip, _, k=k, receiver=receiver, turn=turn):
                first = receiver * CAP + 3 * trip
                cells = cells_v[pl.ds(first + 2, 8, stride=SLOT_ROWS), :]
                lanes, blocks = cells & 127, cells >> 7
                picked = [zeros8] * COMP
                sums = [[zeros8] * COMP for _ in range(2)]
                for step in range(8):
                    one_hot_pair(first + step // 4, step % 4, sums[step // 4])
                    for block in range(16 * step, 16 * step + 16):
                        hit = blocks == block
                        at = (block // 8) * LINE + block % 8
                        for c in range(COMP):
                            values = cur[pl.ds(at + c * 8, 8, stride=0), :]
                            picked[c] = jnp.where(hit, lane_gather(values, lanes), picked[c])
                weight = weights_v[pl.ds(first + 2, 8, stride=SLOT_ROWS), :]
                sums.append([p * weight for p in picked])
                for e in range(3):
                    for c in range(COMP):
                        sent[it, k - 1, trip, e * COMP + c : e * COMP + c + 1, :] = jnp.sum(
                            sums[e][c], axis=0, keepdims=True
                        )
                if it > 0 or turn > 0:
                    slot_copy(it, k, trip).start()
                return 0

            lax.fori_loop(0, CAP // 3, three_rows, 0)
            if it == 0 and turn == 0:
                load_coefficients()
                barrier_wait()
                for half in range(2):
                    slot_copy(it, k, half).start()
                send_matrices()

    def invert_fringe():
        total = jnp.zeros((256, 128), F32)
        lane = iota((128, 128), 1).astype(F32)
        place_of = iota((128, 128), 0)
        for k in ORDER:
            source = lax.rem(g + GRIDS - k, GRIDS)
            named, columns = [], []
            for b in range(CAP):
                row = source * CAP + b
                cell = fringe_v[pl.ds(row, 1), :]
                live = live_v[pl.ds(row, 1), :]
                high = jnp.where(live == 1, cell >> 7, -1)
                low = cell & 127
                hit = place_of == high
                number = float((k - 1) * CAP + b + 1)
                named.append(
                    jnp.concatenate(
                        [jnp.where(hit, number, 0.0), jnp.where(hit, lane, 0.0)], axis=0
                    ).astype(BF16)
                )
                columns.append(jnp.where(place_of == low, 1.0, 0.0).astype(BF16))
            total = total + lax.dot_general(
                jnp.concatenate(named, axis=1),
                jnp.concatenate(columns, axis=1),
                (((1,), (1,)), ((), ())),
                preferred_element_type=F32,
            )
        inverse[...] = total
        inv_row[...] = inverse[0:128, :].astype(jnp.int32) - 1
        inv_lane[...] = inverse[128:256, :].astype(jnp.int32)

    def line(ref, i):
        return ref[i * LINE : i * LINE + LINE, :]

    def block_matrices():
        zero = jnp.zeros((LINE, 128), F32)
        ones = jnp.ones((LINE, 128), F32)
        a1, a2, b1, b2 = ones, zero, zero, ones
        for i in range(ROWS):
            c1, c2 = line(low1, i), line(low2, i)
            a1, a2 = -c1 * a1 - c2 * a2, a1
            b1, b2 = -c1 * b1 - c2 * b2, b1
            one_rows[i * LINE : i * LINE + LINE, :] = a1
            two_rows[i * LINE : i * LINE + LINE, :] = b1
        found = [a1, b1, a2, b2]
        a1, a2, b1, b2 = ones, zero, zero, ones
        p1 = p2 = q1 = q2 = zero
        for i in reversed(range(ROWS)):
            c1, c2, pv = line(up1, i), line(up2, i), line(piv, i)
            a1, a2 = -c1 * a1 - c2 * a2, a1
            b1, b2 = -c1 * b1 - c2 * b2, b1
            p1, p2 = pv * line(one_rows, i) - c1 * p1 - c2 * p2, p1
            q1, q2 = pv * line(two_rows, i) - c1 * q1 - c2 * q2, q1
        found += [a1, b1, a2, b2, p1, q1, p2, q2]
        for c in range(COMP):
            part = [whole[c * 8 : c * 8 + 8, :] for whole in found]
            for j in range(0, 12, 4):
                for half, packed in enumerate(pack(part[j], part[j + 3])):
                    mats[2 * c + half, j // 2] = packed
                for half, packed in enumerate(pack(part[j + 1], part[j + 2])):
                    mats[2 * c + half, j // 2 + 1] = packed

    def load_coefficients():
        for k, lines in ((3, low1), (4, low2), (5, up1), (6, up2), (7, piv)):
            loads[k].wait()
            to_lines(raw.at[k - 2], lines)
        block_matrices()

    def send_matrices():
        for j in visits:

            @pl.when(leader_of(j) != n)
            def _(j=j):
                mat_copy(j).start()

        @pl.when(leader)
        def _():
            mats_in[n] = mats[job]

    def prepare():
        loads[8].wait()
        loads[9].wait()
        invert_fringe()

    def prepare_mixing():
        loads[10].wait()
        loads[11].wait()
        f = [[jnp.broadcast_to(flux_v[k, :, m : m + 1], (8, 128)) for m in range(COMP)] for k in range(COMP)]
        for c in range(COMP):
            row = [left_v[c * COMP + k] for k in range(COMP)]
            for m in range(COMP):
                total = row[0] * f[0][m]
                for k in range(1, COMP):
                    total = total + row[k] * f[k][m]
                mix_c[c * COMP + m] = total * -0.2
                mix_d[c * COMP + m] = row[m] * -0.024

    def place_rows(it, k, half, i_list):
        for i in i_list:
            lanes = inv_lane[i * 8 : i * 8 + 8, :]
            rows = inv_row[i * 8 : i * 8 + 8, :]
            values = [cur[i * LINE + c * 8 : i * LINE + c * 8 + 8, :] for c in range(COMP)]
            for b in range(CAP // 2):
                hit = rows == (k - 1) * CAP + half * (CAP // 2) + b
                for c in range(COMP):
                    slots = received[it, k - 1, half, pl.ds(b * COMP + c, 8, stride=0), :]
                    values[c] = jnp.where(hit, lane_gather(slots, lanes), values[c])
            for c in range(COMP):
                cur[i * LINE + c * 8 : i * LINE + c * 8 + 8, :] = values[c]

    def place(it):
        for turn, k in enumerate(ORDER):
            for half in range(2):
                slot_copy(it, k, half).wait_recv()
                if turn == GRIDS - 2 and half == 1:
                    place_rows(it, k, half, (0, 1, 14, 15))
                    start_z(it)
                    place_rows(it, k, half, range(2, 14))
                else:
                    place_rows(it, k, half, range(ROWS))

    def start_z(it):
        @pl.when(n < NORMALS - 1)
        def _():
            z_copy(it, 0).start()

        @pl.when(n > 0)
        def _():
            z_copy(it, 1).start()

    def start_y(it):
        lane = iota((8, 128), 1)
        for side in range(2):
            total = zeros8
            for m in range(10):
                rows = cur[pl.ds(m * 64 + (7 if side == 0 else 0), 8, stride=8), :]
                shift = (2 * m + (2 if side == 0 else 0)) % 128
                rows = pltpu.roll(rows, shift, 1) if shift else rows
                total = jnp.where((lane >> 1) == m, rows, total)
            ysend[it, side] = total

        @pl.when(s < SPANS - 1)
        def _():
            y_copy(it, 0).start()

        @pl.when(s > 0)
        def _():
            y_copy(it, 1).start()

    def finish_y(it):
        @pl.when(s > 0)
        def _():
            y_copy(it, 0).wait_recv()

        @pl.when(s < SPANS - 1)
        def _():
            y_copy(it, 1).wait_recv()

        for side, halo in ((0, halo_l), (1, halo_r)):
            packed = yrecv[it, side]
            for m in range(10):
                shift = (126 - 2 * m) if side == 0 else (128 - 2 * m) % 128
                halo[m * 8 : m * 8 + 8, :] = pltpu.roll(packed, shift, 1) if shift else packed

    def source_row(it, i):
        lane = iota((8, 128), 1)
        sub = iota((8, 128), 0)

        def at(row, c):
            if row < 0:
                return zlo[it, (row + 2) * LINE + c * 8 : (row + 2) * LINE + c * 8 + 8, :]
            if row >= ROWS:
                return zhi[it, (row - ROWS) * LINE + c * 8 : (row - ROWS) * LINE + c * 8 + 8, :]
            return cur[row * LINE + c * 8 : row * LINE + c * 8 + 8, :]

        central, fourth = [], []
        for c in range(COMP):
            x = at(i, c)
            above = jnp.where(
                sub == 7, halo_r[pl.ds(i * COMP + c, 8, stride=0), :], pltpu.roll(x, 7, 0)
            )
            below = jnp.where(
                sub == 0, halo_l[pl.ds(i * COMP + c, 8, stride=0), :], pltpu.roll(x, 1, 0)
            )
            plus1 = pltpu.roll(jnp.where(lane < 1, above, x), 127, 1)
            plus2 = pltpu.roll(jnp.where(lane < 2, above, x), 126, 1)
            minus1 = pltpu.roll(jnp.where(lane >= 127, below, x), 1, 1)
            minus2 = pltpu.roll(jnp.where(lane >= 126, below, x), 2, 1)
            central.append(plus1 - minus1)
            near = (plus1 + minus1) + (at(i + 1, c) + at(i - 1, c))
            far = (plus2 + minus2) + (at(i + 2, c) + at(i - 2, c))
            fourth.append(far - 4.0 * near + 12.0 * x)
        for c in range(COMP):
            total = mix_c[c * COMP] * central[0] + mix_d[c * COMP] * fourth[0]
            for m in range(1, COMP):
                total = total + mix_c[c * COMP + m] * central[m] + mix_d[c * COMP + m] * fourth[m]
            src[i * LINE + c * 8 : i * LINE + c * 8 + 8, :] = total

    def sweep(e1, e2, f1, f2):
        for i in range(ROWS):
            e1, e2 = line(src, i) - line(low1, i) * e1 - line(low2, i) * e2, e1
            one_rows[i * LINE : i * LINE + LINE, :] = e1
        for i in reversed(range(ROWS)):
            f1, f2 = line(piv, i) * line(one_rows, i) - line(up1, i) * f1 - line(up2, i) * f2, f1
            two_rows[i * LINE : i * LINE + LINE, :] = f1
        return e1, e2, f1, f2

    def lead(it):
        def arrive(k, _):
            @pl.when(k != n)
            def _():
                if it == 0:
                    mat_arrival(k).wait_recv()
                b_arrival(it, k).wait_recv()

            return 0

        lax.fori_loop(0, NORMALS, arrive, 0)
        def apply(k, at, x):
            return mats_in[k, at] * x + mats_in[k, at + 1] * pltpu.roll(x, 4, 0)

        x = zeros8
        pushed = []
        for k in range(NORMALS):
            enter_out[it, k, 0] = x
            pushed.append(apply(k, 4, x) + bounds_in[it, k, 1])
            x = apply(k, 0, x) + bounds_in[it, k, 0]
        x = zeros8
        for k in reversed(range(NORMALS)):
            enter_out[it, k, 1] = x
            x = apply(k, 2, x) + pushed[k]
        for far in range(8, 0, -1):
            for off in {far, NORMALS - far}:
                e_copy(it, lax.rem(n + off, NORMALS)).start()
        enter[it, job] = enter_out[it, n]

    def lines_step(it):
        zero = jnp.zeros((LINE, 128), F32)
        found = sweep(zero, zero, zero, zero)
        for c in range(COMP):
            part = [whole[c * 8 : c * 8 + 8, :] for whole in found]
            for way in range(2):
                for half, packed in enumerate(pack(part[2 * way], part[2 * way + 1])):
                    bounds[it, 2 * c + half, way] = packed
        for j in visits:

            @pl.when(leader_of(j) != n)
            def _(j=j):
                b_copy(it, j).start()

        @pl.when(leader)
        def _():
            bounds_in[it, n] = bounds[it, job]
            lead(it)

        if it == 0:
            finish_loads()
        for j in range(JOBS):

            @pl.when(n != leader_of(j))
            def _(j=j):
                e_arrival(it, j).wait_recv()

        entering = [[], [], [], []]
        for c in range(COMP):
            for way in range(2):
                x, y = pack(enter[it, 2 * c, way], enter[it, 2 * c + 1, way])
                entering[2 * way].append(x)
                entering[2 * way + 1].append(y)
        entering = [jnp.concatenate(parts, axis=0) for parts in entering]
        sweep(*entering)

    def finish_loads():
        loads[12].wait()
        loads[13].wait()
        for half in range(2):
            for a in range(8):
                tile = iblank_v[half * 8 : half * 8 + 8, a * 128 : a * 128 + 128]
                active[pl.ds(half * 64 + a, 8, stride=8), :] = tile.astype(F32)

    def update(it):
        for i in range(ROWS):
            solved = [two_rows[i * LINE + m * 8 : i * LINE + m * 8 + 8, :] for m in range(COMP)]
            mask = active[i * 8 : i * 8 + 8, :]
            for c in range(COMP):
                total = right_v[c * COMP] * solved[0]
                for m in range(1, COMP):
                    total = total + right_v[c * COMP + m] * solved[m]
                at = slice(i * LINE + c * 8, i * LINE + c * 8 + 8)
                cur[at, :] = cur[at, :] + mask * total

    for it in range(ITERS):
        interpolate(it)
        if it == 0:
            prepare()
            prepare_mixing()
        place(it)
        start_y(it)
        finish_y(it)
        for i in range(2, ROWS - 2):
            source_row(it, i)

        @pl.when(n > 0)
        def _(it=it):
            z_copy(it, 0).wait_recv()

        @pl.when(n < NORMALS - 1)
        def _(it=it):
            z_copy(it, 1).wait_recv()

        for i in (0, 1, ROWS - 2, ROWS - 1):
            source_row(it, i)
        lines_step(it)

        @pl.when(n < NORMALS - 1)
        def _(it=it):
            z_copy(it, 0).wait_send()

        @pl.when(n > 0)
        def _(it=it):
            z_copy(it, 1).wait_send()

        update(it)

    for c in range(COMP):
        for half in range(2):
            for a in range(8):
                out[c, half * 8 : half * 8 + 8, a * 128 : a * 128 + 128] = cur[
                    pl.ds(half * 8 * LINE + c * 8 + a, 8, stride=LINE), :
                ]

    for it in range(ITERS):
        for k in ORDER:
            for half in range(2):
                slot_copy(it, k, half).wait_send()

        @pl.when(s < SPANS - 1)
        def _(it=it):
            y_copy(it, 0).wait_send()

        @pl.when(s > 0)
        def _(it=it):
            y_copy(it, 1).wait_send()

        for j in range(JOBS):

            @pl.when(n != leader_of(j))
            def _(j=j, it=it):
                if it == 0:
                    mat_copy(j).wait_send()
                b_copy(it, j).wait_send()

        @pl.when(leader)
        def _(it=it):
            for off in range(1, NORMALS):
                e_copy(it, lax.rem(n + off, NORMALS)).wait_send()


def vmem(*shape, dtype=F32):
    return pltpu.VMEM(shape, dtype)


def local(
    state,
    iblank,
    flux,
    left_vectors,
    right_vectors,
    low_one,
    low_two,
    up_one,
    up_two,
    pivot,
    donor_cells,
    donor_weights,
    fringe_cells,
    fringe_live,
):
    dma = pltpu.SemaphoreType.DMA
    whole = ROWS * LINE
    slots = GRIDS * CAP
    out = pl.pallas_call(
        kernel,
        out_shape=jax.ShapeDtypeStruct((COMP, ROWS, 1024), F32),
        in_specs=[pl.BlockSpec(memory_space=pltpu.HBM)] * 14,
        out_specs=pl.BlockSpec(memory_space=pltpu.VMEM),
        scratch_shapes=[
            vmem(6, COMP, ROWS, 1024),
            vmem(ROWS, 1024, dtype=jnp.int32),
            vmem(COMP, 1, COMP),
            vmem(25, 8, 128),
            vmem(25, 8, 128),
            vmem(8 * slots, 128, dtype=jnp.int32),
            vmem(8 * slots, 128),
            vmem(slots, 128, dtype=jnp.int32),
            vmem(slots, 128, dtype=jnp.int32),
            vmem(whole, 128),
            vmem(whole, 128),
            vmem(whole, 128),
            vmem(whole, 128),
            vmem(whole, 128),
            vmem(whole, 128),
            vmem(ROWS * 8, 128),
            vmem(25, 8, 128),
            vmem(25, 8, 128),
            vmem(whole, 128),
            vmem(whole, 128),
            vmem(whole, 128),
            vmem(320, 512, dtype=BF16),
            vmem(256, 128),
            vmem(128, 128, dtype=jnp.int32),
            vmem(128, 128, dtype=jnp.int32),
            vmem(ITERS, 3, 2, CAP // 2 * COMP, 128),
            vmem(ITERS, 3, 2, CAP // 2 * COMP, 128),
            vmem(ITERS, 2, 8, 128),
            vmem(ITERS, 2, 8, 128),
            vmem(80, 128),
            vmem(80, 128),
            vmem(ITERS, 2 * LINE, 128),
            vmem(ITERS, 2 * LINE, 128),
            vmem(JOBS, 6, 8, 128),
            vmem(NORMALS, 6, 8, 128),
            vmem(ITERS, JOBS, 2, 8, 128),
            vmem(ITERS, NORMALS, 2, 8, 128),
            vmem(ITERS, NORMALS, 2, 8, 128),
            vmem(ITERS, JOBS, 2, 8, 128),
            dma((14,)),
            dma((ITERS, 3, 2)),
            dma((ITERS, 3, 2)),
            dma((ITERS, 2)),
            dma((ITERS, 2)),
            dma((ITERS, 2)),
            dma((ITERS, 2)),
            dma((JOBS,)),
            dma((NORMALS,)),
            dma((ITERS, JOBS)),
            dma((ITERS, NORMALS)),
            dma((ITERS, NORMALS)),
            dma((ITERS, JOBS)),
        ],
        compiler_params=pltpu.CompilerParams(
            collective_id=0, has_side_effects=True, vmem_limit_bytes=48 << 20
        ),
        name="adi_window",
    )(*(pltpu.with_memory_space_constraint(x, pltpu.HBM) for x in (
        state[:, 0],
        iblank[0],
        jnp.swapaxes(flux, 1, 2),
        left_vectors.reshape(25, 8, 128),
        right_vectors.reshape(25, 8, 128),
        low_one[:, 0],
        low_two[:, 0],
        up_one[:, 0],
        up_two[:, 0],
        pivot[:, 0],
        donor_cells.reshape(8 * slots, 128),
        donor_weights.reshape(8 * slots, 128),
        fringe_cells[0],
        fringe_live[0],
    )))
    return out[:, None]


def solution(mesh):
    cells = P(None, "grid", "normal", "span")
    slots = P("grid", "normal", "span")
    lines = P(None, None, "grid", "span")
    return jax.shard_map(
        local,
        mesh=mesh,
        in_specs=(
            cells,
            slots,
            P(None, None, "grid"),
            lines,
            lines,
            cells,
            cells,
            cells,
            cells,
            cells,
            cells,
            cells,
            slots,
            slots,
        ),
        out_specs=cells,
        check_vma=False,
    )
```
